32 devices in a mesh: sec: 4 (over y, core), ctx: 2 (over x), tp: 4 (over z).
Axes of the slice: x: 2, y: 2, z: 4, core: 2. Of those that a mesh axis runs over, the one named last changes fastest.
Arguments:
- self_query: bfloat16 [1024, 2048], P('ctx', ('sec', 'tp')), may hold values from -6 to 6
- self_key: bfloat16 [1024, 2048], P('ctx', ('sec', 'tp')), may hold values from -6 to 6
- self_value: bfloat16 [1024, 2048], P('ctx', ('sec', 'tp')), may hold values from -6 to 6
- self_gain: float32 [2048], P(('sec', 'tp')), may hold values from 0.5 to 1.5
- self_grad: bfloat16 [1024, 2048], P('ctx', ('sec', 'tp')), may hold values from -6 to 6
- cross_query: bfloat16 [1024, 2048], P('ctx', ('sec', 'tp')), may hold values from -6 to 6
- memory_key: bfloat16 [256, 2048], P(('sec', 'ctx')), may hold values from -6 to 6
- memory_value: bfloat16 [256, 2048], P(('sec', 'ctx')), may hold values from -6 to 6
- cross_gain: float32 [2048], P(('sec', 'tp')), may hold values from 0.5 to 1.5
- cross_grad: bfloat16 [1024, 2048], P('ctx', ('sec', 'tp')), may hold values from -6 to 6
- block_start: int32 [8], replicated, may hold values from 0 to 7, each once
Outputs:
- self_out: bfloat16 [1024, 2048], P('ctx', ('sec', 'tp'))
- cross_out: bfloat16 [1024, 2048], P('ctx', ('sec', 'tp'))
- query_grad: bfloat16 [1024, 2048], P('ctx', ('sec', 'tp'))
- key_grad: bfloat16 [1024, 2048], P('ctx', ('sec', 'tp'))
- value_grad: bfloat16 [1024, 2048], P('ctx', ('sec', 'tp'))
- cross_query_grad: bfloat16 [1024, 2048], P('ctx', ('sec', 'tp'))
- memory_key_grad: bfloat16 [256, 2048], P(('sec', 'ctx'))
- memory_value_grad: bfloat16 [256, 2048], P(('sec', 'ctx'))
The draws below stay inside these ranges and needn't reach their ends.
Inputs may be any that keep to these rules, and one draw needn't show every extreme that they name: `block_start`: every number appears once.
All inputs are finite; a program needn't handle non-finite values.
Results may differ from the reference program's by a relative error of at most 0.015.
Values may be sent and summed in bfloat16 or wider, within the bound.
No kernel may reach another device: no remote copies, remote signals or barrier semaphores. Data moves between devices by JAX's collectives and lax.ppermute only.
A program may use at most 64 MiB of HBM per device.

```python
import math
import jax
import jax.numpy as jnp
from jax import lax

HEADS = 16
HEAD_DIM = 128
FR_DEV = 512
FRAMES = 1024
MEMORY = 256
N_CTX = 2


def base_draw(key, row_count):
    return jnp.clip(jax.random.normal(key, (row_count, HEADS * HEAD_DIM), jnp.float32), -6.0, 6.0)


def head_scales():
    head_ids = jnp.arange(HEADS * HEAD_DIM) // HEAD_DIM
    position_ratio = head_ids.astype(jnp.float32) / max(HEADS - 1, 1)
    return 3.0 ** position_ratio / 1.7


def value_draw(key, row_count):
    base_values = jax.random.normal(key, (row_count, HEADS * HEAD_DIM), jnp.float32)
    return jnp.clip(base_values * head_scales()[None, :], -6.0, 6.0)


def draw_self_query(key, part):
    drawn = base_draw(jax.random.fold_in(key, 101), FRAMES)
    return drawn.astype(jnp.bfloat16)


def draw_self_key(key, part):
    drawn = base_draw(jax.random.fold_in(key, 102), FRAMES)
    return drawn.astype(jnp.bfloat16)


def draw_self_value(key, part):
    return value_draw(jax.random.fold_in(key, 103), FRAMES).astype(jnp.bfloat16)


def draw_cross_query(key, part):
    drawn = base_draw(jax.random.fold_in(key, 104), FRAMES)
    return drawn.astype(jnp.bfloat16)


def draw_memory_key(key, part):
    drawn = base_draw(jax.random.fold_in(key, 105), MEMORY)
    return drawn.astype(jnp.bfloat16)


def draw_memory_value(key, part):
    return value_draw(jax.random.fold_in(key, 106), MEMORY).astype(jnp.bfloat16)


def steps_of(stream_key, shape, shards, least, top_value):
    level, own = 1.0, jax.random.fold_in(stream_key, 6)
    for axis_at, parts in shards:
        heights = jnp.exp(jax.random.uniform(jax.random.fold_in(own, axis_at), (parts,), jnp.float32, least / len(shards), top_value / len(shards)))
        level = level * jnp.repeat(heights, shape[axis_at] // parts).reshape([-1 if axis == axis_at else 1 for axis in range(len(shape))])
    return level


def noise(stream_key, shape, width, bound, pieces=(), kind=jnp.bfloat16):
    level = steps_of(stream_key, shape, pieces, -0.22, 0.18) if pieces else 1.0
    values = jax.random.normal(stream_key, shape, jnp.float32) * width * level
    return jnp.minimum(jnp.maximum(values, -bound), bound).astype(kind)


def setup_inputs(seed: int = 0) -> dict:
    splits = jax.random.split(jax.random.key(seed), 12)
    self_query = draw_self_query(jax.random.fold_in(splits[11], 71), 0)
    self_key = draw_self_key(jax.random.fold_in(splits[11], 71), 0)
    self_value = draw_self_value(jax.random.fold_in(splits[11], 71), 0)
    self_gain = jnp.clip(1.0 + 0.1 * jax.random.normal(splits[3], (HEADS * HEAD_DIM,), jnp.float32), 0.5, 1.5)
    self_grad = noise(splits[4], (FRAMES, HEADS * HEAD_DIM), 1.0, 6.0, ((0, 2), (1, 16)))
    cross_query = draw_cross_query(jax.random.fold_in(splits[11], 71), 0)
    memory_key = draw_memory_key(jax.random.fold_in(splits[11], 71), 0)
    memory_value = draw_memory_value(jax.random.fold_in(splits[11], 71), 0)
    cross_gain = jnp.clip(1.0 + 0.1 * jax.random.normal(splits[8], (HEADS * HEAD_DIM,), jnp.float32), 0.5, 1.5)
    cross_grad = noise(splits[9], (FRAMES, HEADS * HEAD_DIM), 1.0, 6.0, ((0, 2), (1, 16)))
    block_start = jax.random.permutation(splits[10], 4 * N_CTX).astype(jnp.int32)
    return dict(self_query=self_query, self_key=self_key, self_value=self_value, self_gain=self_gain, self_grad=self_grad, cross_query=cross_query, memory_key=memory_key, memory_value=memory_value, cross_gain=cross_gain, cross_grad=cross_grad, block_start=block_start)


EPS = 1e-06

def heads_first(matrix):
    return matrix.reshape(matrix.shape[0], HEADS, HEAD_DIM).transpose(1, 0, 2)

def heads_last(stacked):
    return stacked.transpose(1, 0, 2).reshape(stacked.shape[1], HEADS * HEAD_DIM)

def in_blocks(tensor_in, block_rows):
    return tensor_in.reshape((tensor_in.shape[0] // block_rows, block_rows) + tensor_in.shape[1:])

def head_scores(queries, key_rows, query_position, key_position, causal):
    scores = jnp.dot(queries, key_rows.T, preferred_element_type=jnp.float32) * (1.0 / math.sqrt(HEAD_DIM))
    if causal:
        scores = jnp.where(key_position[None, :] > query_position[:, None], -jnp.inf, scores)
    return scores

def forward_head(queries, key_rows, value_rows, query_position, key_position, causal, block_rows):

    def one_block(packed):
        block_queries, block_position = packed
        scores = head_scores(block_queries, key_rows, block_position, key_position, causal)
        row_top = lax.optimization_barrier(jnp.max(scores, axis=1))
        log_total = row_top + jnp.log(lax.optimization_barrier(jnp.sum(jnp.exp(scores - row_top[:, None]), axis=1)))
        weights = jnp.exp(scores - log_total[:, None]).astype(jnp.bfloat16)
        return (log_total, jnp.dot(weights, value_rows, preferred_element_type=jnp.float32))
    log_total, attended = lax.map(one_block, (in_blocks(queries, block_rows), in_blocks(query_position, block_rows)))
    return (log_total.reshape(-1), attended.reshape(-1, HEAD_DIM))

def backward_head(queries, key_rows, value_rows, cotangent, attended, log_total, query_position, key_position, causal, block_rows):
    row_delta = lax.optimization_barrier(jnp.sum(cotangent.astype(jnp.float32) * attended, axis=1))
    scaling = 1.0 / math.sqrt(HEAD_DIM)

    def one_block(carried, packed):
        key_sum, value_sum = carried
        block_queries, block_grad, block_total, block_delta, block_position = packed
        scores = head_scores(block_queries, key_rows, block_position, key_position, causal)
        weights = jnp.exp(scores - block_total[:, None])
        products = jnp.dot(block_grad, value_rows.T, preferred_element_type=jnp.float32)
        score_grad = (weights * (products - block_delta[:, None])).astype(jnp.bfloat16)
        query_part = jnp.dot(score_grad, key_rows, preferred_element_type=jnp.float32) * scaling
        key_sum = key_sum + jnp.dot(score_grad.T, block_queries, preferred_element_type=jnp.float32) * scaling
        value_sum = value_sum + jnp.dot(weights.astype(jnp.bfloat16).T, block_grad, preferred_element_type=jnp.float32)
        return ((key_sum, value_sum), query_part)
    zeros = jnp.zeros(key_rows.shape, jnp.float32)
    packed = (in_blocks(queries, block_rows), in_blocks(cotangent, block_rows), in_blocks(log_total, block_rows), in_blocks(row_delta, block_rows), in_blocks(query_position, block_rows))
    (key_sum, value_sum), query_part = lax.scan(one_block, (zeros, zeros), packed)
    return (query_part.reshape(-1, HEAD_DIM), key_sum, value_sum)

def attention_part(queries, key_rows, value_rows, gain, cotangent, query_position, key_position, causal):
    block_rows = math.gcd(FRAMES, 1024)
    query_heads = heads_first(queries)
    key_heads = heads_first(key_rows)
    value_heads = heads_first(value_rows)

    def forward_one(packed):
        return forward_head(packed[0], packed[1], packed[2], query_position, key_position, causal, block_rows)
    log_total, attended = lax.map(forward_one, (query_heads, key_heads, value_heads))
    flattened = heads_last(attended)
    row_scale = lax.rsqrt(lax.optimization_barrier(jnp.mean(flattened * flattened, axis=1)) + EPS)
    output = (gain[None, :] * flattened * row_scale[:, None]).astype(jnp.bfloat16)
    lifted = gain[None, :] * cotangent.astype(jnp.float32)
    row_slope = lax.optimization_barrier(jnp.mean(lifted * flattened, axis=1))
    attended_grad = (row_scale[:, None] * (lifted - flattened * (row_scale * row_scale * row_slope)[:, None])).astype(jnp.bfloat16)
    grad_heads = heads_first(attended_grad)

    def backward_one(packed):
        return backward_head(packed[0], packed[1], packed[2], packed[3], packed[4], packed[5], query_position, key_position, causal, block_rows)
    query_part, key_part, value_part = lax.map(backward_one, (query_heads, key_heads, value_heads, grad_heads, attended, log_total))
    return (output, heads_last(query_part).astype(jnp.bfloat16), heads_last(key_part).astype(jnp.bfloat16), heads_last(value_part).astype(jnp.bfloat16))

def reference(self_query, self_key, self_value, self_gain, self_grad, cross_query, memory_key, memory_value, cross_gain, cross_grad, block_start):
    quarter = FR_DEV // 4
    row_ids = jnp.arange(FRAMES, dtype=jnp.int32)
    position = (block_start[row_ids // quarter] * quarter + row_ids % quarter).astype(jnp.int32)
    memory_position = jnp.zeros((MEMORY,), jnp.int32)
    self_out, query_grad, key_grad, value_grad = attention_part(self_query, self_key, self_value, self_gain, self_grad, position, position, True)
    cross_out, cross_query_grad, memory_key_grad, memory_value_grad = attention_part(cross_query, memory_key, memory_value, cross_gain, cross_grad, position, memory_position, False)
    return (self_out, cross_out, query_grad, key_grad, value_grad, cross_query_grad, memory_key_grad, memory_value_grad)
```

```python
import functools
import math

import jax
import jax.numpy as jnp
from jax import lax
from jax.experimental import pallas as pl
from jax.experimental.pallas import tpu as pltpu
from jax.sharding import PartitionSpec as P

EPS = 1e-06
F32 = jnp.float32
BF16 = jnp.bfloat16
VMEM = pl.BlockSpec(memory_space=pltpu.VMEM)
SMEM = pl.BlockSpec(memory_space=pltpu.SMEM)


def call(body, inputs, outputs, flops=0, scratch=(), smem=0, name=None):
    moved = sum(math.prod(shape) * jnp.dtype(kind).itemsize for shape, kind in outputs)
    moved += sum(entry.size * entry.dtype.itemsize for entry in inputs)
    return pl.pallas_call(
        body,
        out_shape=[jax.ShapeDtypeStruct(shape, kind) for shape, kind in outputs],
        in_specs=[SMEM] * smem + [VMEM] * (len(inputs) - smem),
        out_specs=[VMEM] * len(outputs),
        scratch_shapes=list(scratch),
        cost_estimate=pl.CostEstimate(flops=flops, bytes_accessed=moved, transcendentals=0),
        name=name,
    )(*inputs)


def dot_nt(left, right):
    return lax.dot_general(left, right, (((1,), (1,)), ((), ())), preferred_element_type=F32)


def dot_nn(left, right):
    return lax.dot_general(left, right, (((1,), (0,)), ((), ())), preferred_element_type=F32)


def dot_tn(left, right):
    return lax.dot_general(left, right, (((0,), (0,)), ((), ())), preferred_element_type=F32)


def row_positions(starts, first, quarter):
    lanes = lax.broadcasted_iota(jnp.int32, (1, quarter), 1)
    return jnp.concatenate([starts[first + part] * quarter + lanes for part in range(4)], axis=1)


def fold_block(key, value, queries, running, store, masks, held, scaling):
    rows, step = key.shape[0], 128
    step = min(step, rows)
    top, total, weighted = running
    block_top = top
    for at in range(0, rows, step):
        scores = dot_nt(key[at : at + step, :], queries) * scaling
        if masks is not None:
            key_first, query_positions = masks
            down = lax.broadcasted_iota(jnp.int32, (step, 1), 0) + key_first(at)
            scores = jnp.where(down > query_positions, -jnp.inf, scores)
        held[at : at + step, :] = scores
        block_max = jnp.max(scores, axis=0, keepdims=True)
        block_top = block_max if block_top is None else jnp.maximum(block_top, block_max)
    block_total = None
    for at in range(0, rows, step):
        raised = jnp.exp(held[at : at + step, :] - block_top)
        part = jnp.sum(raised, axis=0, keepdims=True)
        block_total = part if block_total is None else block_total + part
        store[at : at + step, :] = raised.astype(BF16)
    product = dot_tn(value[...], store[...])
    if top is None:
        return block_top, block_total, product
    shrink = jnp.exp(top - block_top)
    return block_top, total * shrink + block_total, weighted * shrink + product


def solution(mesh):
    sections, contexts, tensors = mesh.shape["sec"], mesh.shape["ctx"], mesh.shape["tp"]
    peers = sections * tensors

    def shifted(value, axis, count, by):
        return lax.ppermute(value, axis, [(at, (at + by) % count) for at in range(count)])

    def per_device(
        self_query,
        self_key,
        self_value,
        self_gain,
        self_grad,
        cross_query,
        memory_key,
        memory_value,
        cross_gain,
        cross_grad,
        block_start,
    ):
        frames, columns = self_query.shape
        rows = memory_key.shape[0]
        quarter = frames // 4
        full_width = columns * peers
        group = sections * rows
        others = contexts - 1
        scaling = 1.0 / math.sqrt(columns)
        wide = (frames, columns)
        tall = (columns, frames)
        line = (1, frames)
        unit = 2 * frames * columns

        other_keys = [shifted(self_key, "ctx", contexts, by) for by in range(1, contexts)]
        other_values = [shifted(self_value, "ctx", contexts, by) for by in range(1, contexts)]

        def prepare(key_ref, value_ref, *outs):
            section, tensor = lax.axis_index("sec"), lax.axis_index("tp")
            for by, out in enumerate(outs):
                head = lax.rem(section + by, sections) * tensors + tensor
                at = pl.ds(pl.multiple_of(head * columns, columns), columns)
                out[0] = key_ref[:, at]
                out[1] = value_ref[:, at]

        pieces = call(
            prepare, [memory_key, memory_value], [((2, rows, columns), BF16)] * sections, name="prepare"
        )
        arrived = [pieces[0]] + [
            shifted(pieces[by], "sec", sections, by) for by in range(1, sections)
        ]

        def gather(*refs):
            out = refs[-1]
            for at, ref in enumerate(refs[:-1]):
                out[:, at * rows : (at + 1) * rows, :] = ref[...]

        (own_memory,) = call(gather, arrived, [((2, group, columns), BF16)], name="gather")
        memories = [own_memory] + [
            shifted(own_memory, "ctx", contexts, by) for by in range(1, contexts)
        ]

        def first_block(starts, query, key, value, gain, grad, store, top, total, weighted, lifted, held):
            context = lax.axis_index("ctx")
            positions = row_positions(starts, context * 4, quarter)
            masks = (
                lambda at: starts[context * 4 + at // quarter] * quarter + at % quarter,
                positions,
            )
            top[...], total[...], weighted[...] = fold_block(
                key, value, query[...], (None, None, None), store, masks, held, scaling
            )
            lifted[...] = (gain[...] * grad[...].astype(F32)).T

        first_store, first_top, first_total, first_weighted, self_lifted = call(
            first_block,
            [block_start, self_query, self_key, self_value, self_gain.reshape(1, columns), self_grad],
            [((frames, frames), BF16), (line, F32), (line, F32), (tall, F32), (tall, F32)],
            flops=2 * frames * unit,
            scratch=[pltpu.VMEM((frames, frames), F32)],
            smem=1,
            name="first_block",
        )

        def statistics(attended, lifted):
            return (
                jnp.sum(attended * attended, axis=0, keepdims=True),
                jnp.sum(lifted * attended, axis=0, keepdims=True),
            )

        def other_blocks(starts, query, top, total, weighted, lifted, *refs):
            keys, values = refs[:others], refs[others : 2 * others]
            stores = refs[2 * others : 3 * others]
            first_weight, weight, attended_ref, stats, held = refs[3 * others :]
            context = lax.axis_index("ctx")
            positions = row_positions(starts, context * 4, quarter)
            running = (top[...], total[...], weighted[...])
            tops = [top[...]]
            for by in range(others):
                source = lax.rem(context - (by + 1) + contexts, contexts)
                masks = (
                    lambda at, source=source: starts[source * 4 + at // quarter] * quarter
                    + at % quarter,
                    positions,
                )
                running = fold_block(
                    keys[by], values[by], query[...], running, stores[by], masks, held, scaling
                )
                tops.append(running[0])
            last = 1.0 / running[1]
            first_weight[...] = jnp.exp(tops[0] - running[0]) * last
            for by in range(others):
                weight[by : by + 1, :] = jnp.exp(tops[by + 1] - running[0]) * last
            attended = running[2] * last
            attended_ref[...] = attended
            stats[0:1, :], stats[1:2, :] = statistics(attended, lifted[...])

        results = call(
            other_blocks,
            [block_start, self_query, first_top, first_total, first_weighted, self_lifted]
            + other_keys
            + other_values,
            [((frames, frames), BF16)] * others
            + [(line, F32), ((others, frames), F32), (tall, F32), ((2, frames), F32)],
            flops=2 * frames * unit * others,
            scratch=[pltpu.VMEM((frames, frames), F32)],
            smem=1,
            name="other_blocks",
        )
        other_stores = results[:others]
        first_weight, other_weight, self_attended, self_stats = results[others:]

        half = frames // 2

        def cross_forward(query, gain, grad, self_stats_ref, *refs):
            blocks, stores = refs[:contexts], refs[contexts : 2 * contexts]
            weight, attended_ref, lifted_ref, stats, packed, held = refs[2 * contexts :]
            running = (None, None, None)
            tops = []
            for at in range(contexts):
                running = fold_block(
                    blocks[at].at[0], blocks[at].at[1], query[...], running, stores[at], None, held, scaling
                )
                tops.append(running[0])
            last = 1.0 / running[1]
            for at in range(contexts):
                weight[at : at + 1, :] = jnp.exp(tops[at] - running[0]) * last
            attended = running[2] * last
            lifted = (gain[...] * grad[...].astype(F32)).T
            attended_ref[...] = attended
            lifted_ref[...] = lifted
            squares, slopes = statistics(attended, lifted)
            stats[0:1, :], stats[1:2, :] = squares, slopes
            lines = [self_stats_ref[0:1, :], self_stats_ref[1:2, :], squares, slopes]
            halves = [entry[:, at : at + half] for entry in lines for at in (0, half)]
            tile = jnp.concatenate(halves, axis=0)
            for at in range(peers):
                packed[at] = tile

        results = call(
            cross_forward,
            [cross_query, cross_gain.reshape(1, columns), cross_grad, self_stats] + memories,
            [((group, frames), BF16)] * contexts
            + [
                ((contexts, frames), F32),
                (tall, F32),
                (tall, F32),
                ((2, frames), F32),
                ((peers, 8, half), F32),
            ],
            flops=2 * group * contexts * unit,
            scratch=[pltpu.VMEM((group, frames), F32)],
            name="cross_forward",
        )
        cross_stores = results[:contexts]
        cross_weight, cross_attended, cross_lifted, cross_stats, packed = results[contexts:]

        received = lax.all_to_all(packed, ("sec", "tp"), split_axis=0, concat_axis=0, tiled=True)

        def norm_terms(received_ref, stats, attended, lifted, at):
            sums = received_ref[0]
            for source in range(1, peers):
                sums = sums + received_ref[source]
            joined = [
                jnp.concatenate([sums[2 * pick : 2 * pick + 1], sums[2 * pick + 1 : 2 * pick + 2]], axis=1)
                for pick in (2 * at, 2 * at + 1)
            ]
            scale = lax.rsqrt(joined[0] / full_width + EPS)
            slope = joined[1] / full_width
            curve = scale * scale * slope
            grad = scale * (lifted[...] - attended[...] * curve)
            delta = scale * (stats[1:2, :] - curve * stats[0:1, :])
            return scale, delta, grad

        def block_grads(key_grad, value_grad, value, store, weight, delta, grad_tall, grad_wide, query, slopes):
            count, step = value.shape[0], 128
            step = min(step, count)
            for at in range(0, count, step):
                products = dot_nn(value[at : at + step, :], grad_tall)
                probs = store[at : at + step, :]
                slope = (probs.astype(F32) * ((products - delta) * weight)).astype(BF16)
                slopes[at : at + step, :] = slope
                key_grad(at, step, dot_nn(slope, query) * scaling)
                value_grad(at, step, dot_nn(probs, grad_wide))

        def cross_backward(received_ref, stats, attended, lifted, weight, query, *refs):
            blocks, stores = refs[:contexts], refs[contexts : 2 * contexts]
            sums, slopes, scale_ref = refs[2 * contexts : 3 * contexts], refs[3 * contexts : 4 * contexts], refs[-1]
            scale, delta, grad = norm_terms(received_ref, stats, attended, lifted, 1)
            scale_ref[...] = scale
            grad_tall = grad.astype(BF16)
            for at in range(contexts):
                line_weight = weight[at : at + 1, :]
                grad_wide = (grad * line_weight).T.astype(BF16)

                def key_grad(first, count, value, out=sums[at]):
                    out[0, first : first + count, :] = value.astype(out.dtype)

                def value_grad(first, count, value, out=sums[at]):
                    out[1, first : first + count, :] = value.astype(out.dtype)

                block_grads(
                    key_grad,
                    value_grad,
                    blocks[at].at[1],
                    stores[at],
                    line_weight,
                    delta,
                    grad_tall,
                    grad_wide,
                    query[...],
                    slopes[at],
                )

        results = call(
            cross_backward,
            [received, cross_stats, cross_attended, cross_lifted, cross_weight, cross_query]
            + memories
            + list(cross_stores),
            [((2, group, columns), F32)]
            + [((2, group, columns), BF16)] * others
            + [((group, frames), BF16)] * contexts
            + [(line, F32)],
            flops=3 * group * contexts * unit,
            name="cross_backward",
        )
        memory_sums, cross_slopes, cross_scale = results[:contexts], results[contexts:-1], results[-1]

        returned = [
            shifted(memory_sums[by], "ctx", contexts, -by) for by in range(1, contexts)
        ]

        def add_up(*refs):
            own, extra, outs = refs[0], refs[1 : 1 + others], refs[1 + others :]
            for at, out in enumerate(outs):
                part = slice(at * rows, (at + 1) * rows)
                total = own[:, part, :]
                for entry in extra:
                    total = total + entry[:, part, :].astype(F32)
                out[...] = total.astype(BF16)

        parts = call(
            add_up, [memory_sums[0]] + returned, [((2, rows, columns), BF16)] * sections, name="add_up"
        )
        back = [parts[0]] + [shifted(parts[by], "sec", sections, -by) for by in range(1, sections)]

        def by_section(*refs):
            out = refs[-1]
            section = lax.axis_index("sec")
            for by, ref in enumerate(refs[:-1]):
                out[lax.rem(section + by, sections)] = ref[...]

        (mine,) = call(by_section, back, [((sections, 2, rows, columns), BF16)], name="by_section")
        lines = [mine] + [shifted(mine, "tp", tensors, by) for by in range(1, tensors)]

        def assemble(*refs):
            sources, key_out, value_out = refs[:tensors], refs[tensors], refs[tensors + 1]
            tensor = lax.axis_index("tp")
            for by, ref in enumerate(sources):
                source = lax.rem(tensor - by + tensors, tensors)
                for section in range(sections):
                    head = section * tensors + source
                    at = pl.ds(pl.multiple_of(head * columns, columns), columns)
                    key_out[:, at] = ref[section, 0]
                    value_out[:, at] = ref[section, 1]

        memory_key_grad, memory_value_grad = call(
            assemble, lines, [(memory_key.shape, BF16), (memory_value.shape, BF16)], name="assemble"
        )

        def other_backward(received_ref, stats, attended, lifted, weight, query, *refs):
            values, stores = refs[:others], refs[others : 2 * others]
            keys_out, values_out = refs[2 * others : 3 * others], refs[3 * others : 4 * others]
            slopes = refs[4 * others : 5 * others]
            grad_ref, scale_ref, delta_ref = refs[5 * others :]
            scale, delta, grad = norm_terms(received_ref, stats, attended, lifted, 0)
            scale_ref[...], delta_ref[...], grad_ref[...] = scale, delta, grad
            grad_tall = grad.astype(BF16)
            for by in range(others):
                line_weight = weight[by : by + 1, :]
                grad_wide = (grad * line_weight).T.astype(BF16)

                def key_grad(first, count, value, out=keys_out[by]):
                    out[first : first + count, :] = value.astype(BF16)

                def value_grad(first, count, value, out=values_out[by]):
                    out[first : first + count, :] = value.astype(BF16)

                block_grads(
                    key_grad,
                    value_grad,
                    values[by],
                    stores[by],
                    line_weight,
                    delta,
                    grad_tall,
                    grad_wide,
                    query[...],
                    slopes[by],
                )

        results = call(
            other_backward,
            [received, self_stats, self_attended, self_lifted, other_weight, self_query]
            + other_values
            + list(other_stores),
            [(wide, BF16)] * (2 * others)
            + [((frames, frames), BF16)] * others
            + [(tall, F32), (line, F32), (line, F32)],
            flops=3 * frames * unit * others,
            name="other_backward",
        )
        away_keys, away_values = results[:others], results[others : 2 * others]
        other_slopes = results[2 * others : 3 * others]
        self_attended_grad, self_scale, self_delta = results[3 * others :]
        home_keys = [shifted(away_keys[by], "ctx", contexts, -(by + 1)) for by in range(others)]
        home_values = [shifted(away_values[by], "ctx", contexts, -(by + 1)) for by in range(others)]

        def own_backward(grad, scale, delta, weight, gain, attended, query, key, value, store, *refs):
            keys, slopes = refs[:others], refs[others : 2 * others]
            key_out, value_out, query_out, out, own_slopes = refs[2 * others :]
            grad_tall = grad[...].astype(BF16)
            line_weight = weight[...]
            grad_wide = (grad[...] * line_weight).T.astype(BF16)

            def key_grad(first, count, result):
                key_out[first : first + count, :] = result

            def value_grad(first, count, result):
                value_out[first : first + count, :] = result

            block_grads(
                key_grad,
                value_grad,
                value,
                store,
                line_weight,
                delta[...],
                grad_tall,
                grad_wide,
                query[...],
                own_slopes,
            )
            total = dot_tn(key[...], own_slopes[...])
            for by in range(others):
                total = total + dot_tn(keys[by][...], slopes[by][...])
            query_out[...] = (total * scaling).T.astype(BF16)
            out[...] = (gain[...] * (attended[...] * scale[...]).T).astype(BF16)

        own_key, own_value, query_grad, self_out = call(
            own_backward,
            [
                self_attended_grad,
                self_scale,
                self_delta,
                first_weight,
                self_gain.reshape(1, columns),
                self_attended,
                self_query,
                self_key,
                self_value,
                first_store,
            ]
            + other_keys
            + list(other_slopes),
            [(wide, F32), (wide, F32), (wide, BF16), (wide, BF16)],
            flops=(4 + others) * frames * unit,
            scratch=[pltpu.VMEM((frames, frames), BF16)],
            name="own_backward",
        )

        def cross_rest(scale, gain, attended, *refs):
            blocks, slopes = refs[:contexts], refs[contexts : 2 * contexts]
            query_out, out = refs[2 * contexts :]
            total = dot_tn(blocks[0][0], slopes[0][...])
            for at in range(1, contexts):
                total = total + dot_tn(blocks[at][0], slopes[at][...])
            query_out[...] = (total * scaling).T.astype(BF16)
            out[...] = (gain[...] * (attended[...] * scale[...]).T).astype(BF16)

        cross_query_grad, cross_out = call(
            cross_rest,
            [cross_scale, cross_gain.reshape(1, columns), cross_attended] + memories + list(cross_slopes),
            [(wide, BF16), (wide, BF16)],
            flops=group * contexts * unit,
            name="cross_rest",
        )

        key_grad = own_key
        value_grad = own_value
        for by in range(others):
            key_grad = key_grad + home_keys[by].astype(F32)
            value_grad = value_grad + home_values[by].astype(F32)
        return (
            self_out,
            cross_out,
            query_grad,
            key_grad.astype(BF16),
            value_grad.astype(BF16),
            cross_query_grad,
            memory_key_grad,
            memory_value_grad,
        )

    rowed = P("ctx", ("sec", "tp"))
    stored = P(("sec", "ctx"), None)
    gains = P(("sec", "tp"))
    return jax.shard_map(
        per_device,
        mesh=mesh,
        in_specs=(rowed, rowed, rowed, gains, rowed, rowed, stored, stored, gains, rowed, P()),
        out_specs=(rowed, rowed, rowed, rowed, rowed, rowed, stored, stored),
        check_vma=False,
    )
```

```python
import functools
import math

import jax
import jax.numpy as jnp
from jax import lax
from jax.experimental import pallas as pl
from jax.experimental.pallas import tpu as pltpu
from jax.sharding import PartitionSpec as P

EPS = 1e-06
F32 = jnp.float32
BF16 = jnp.bfloat16
VMEM = pl.BlockSpec(memory_space=pltpu.VMEM)
ROOM = 4 << 20
LIMIT = 60 << 20
SMEM = pl.BlockSpec(memory_space=pltpu.SMEM)


def call(body, inputs, outputs, flops=0, scratch=(), smem=0, name=None):
    moved = sum(math.prod(shape) * jnp.dtype(kind).itemsize for shape, kind in outputs)
    moved += sum(entry.size * entry.dtype.itemsize for entry in inputs)
    held = sum(math.prod(entry.shape) * jnp.dtype(entry.dtype).itemsize for entry in scratch)
    return pl.pallas_call(
        body,
        out_shape=[jax.ShapeDtypeStruct(shape, kind) for shape, kind in outputs],
        in_specs=[SMEM] * smem + [VMEM] * (len(inputs) - smem),
        out_specs=[VMEM] * len(outputs),
        scratch_shapes=list(scratch),
        cost_estimate=pl.CostEstimate(flops=flops, bytes_accessed=moved, transcendentals=0),
        compiler_params=pltpu.CompilerParams(vmem_limit_bytes=min(2 * (moved + held) + ROOM, LIMIT)),
        name=name,
    )(*inputs)


def dot_nt(left, right):
    return lax.dot_general(left, right, (((1,), (1,)), ((), ())), preferred_element_type=F32)


def dot_nn(left, right):
    return lax.dot_general(left, right, (((1,), (0,)), ((), ())), preferred_element_type=F32)


def dot_tn(left, right):
    return lax.dot_general(left, right, (((0,), (0,)), ((), ())), preferred_element_type=F32)


def row_positions(starts, first, quarter):
    lanes = lax.broadcasted_iota(jnp.int32, (1, quarter), 1)
    return jnp.concatenate([starts[first + part] * quarter + lanes for part in range(4)], axis=1)


def fold_block(key, value, queries, running, store, masks, held, scaling):
    rows, step = key.shape[0], 128
    step = min(step, rows)
    top, total, weighted = running
    block_top = top
    for at in range(0, rows, step):
        scores = dot_nt(key[at : at + step, :], queries) * scaling
        if masks is not None:
            key_first, query_positions = masks
            down = lax.broadcasted_iota(jnp.int32, (step, 1), 0) + key_first(at)
            scores = jnp.where(down > query_positions, -jnp.inf, scores)
        held[at : at + step, :] = scores
        block_max = jnp.max(scores, axis=0, keepdims=True)
        block_top = block_max if block_top is None else jnp.maximum(block_top, block_max)
    block_total = None
    for at in range(0, rows, step):
        raised = jnp.exp(held[at : at + step, :] - block_top)
        part = jnp.sum(raised, axis=0, keepdims=True)
        block_total = part if block_total is None else block_total + part
        store[at : at + step, :] = raised.astype(BF16)
    product = dot_tn(value[...], store[...])
    if top is None:
        return block_top, block_total, product
    shrink = jnp.exp(top - block_top)
    return block_top, total * shrink + block_total, weighted * shrink + product


def solution(mesh):
    sections, contexts, tensors = mesh.shape["sec"], mesh.shape["ctx"], mesh.shape["tp"]
    peers = sections * tensors

    def shifted(value, axis, count, by):
        return lax.ppermute(value, axis, [(at, (at + by) % count) for at in range(count)])

    def per_device(
        self_query,
        self_key,
        self_value,
        self_gain,
        self_grad,
        cross_query,
        memory_key,
        memory_value,
        cross_gain,
        cross_grad,
        block_start,
    ):
        frames, columns = self_query.shape
        rows = memory_key.shape[0]
        quarter = frames // 4
        full_width = columns * peers
        group = sections * rows
        others = contexts - 1
        scaling = 1.0 / math.sqrt(columns)
        wide = (frames, columns)
        tall = (columns, frames)
        line = (1, frames)
        unit = 2 * frames * columns

        other_keys = [shifted(self_key, "ctx", contexts, by) for by in range(1, contexts)]
        other_values = [shifted(self_value, "ctx", contexts, by) for by in range(1, contexts)]

        def prepare(key_ref, value_ref, *outs):
            section, tensor = lax.axis_index("sec"), lax.axis_index("tp")
            for by, out in enumerate(outs):
                head = lax.rem(section + by, sections) * tensors + tensor
                at = pl.ds(pl.multiple_of(head * columns, columns), columns)
                out[0] = key_ref[:, at]
                out[1] = value_ref[:, at]

        pieces = call(
            prepare, [memory_key, memory_value], [((2, rows, columns), BF16)] * sections, name="prepare"
        )
        arrived = [pieces[0]] + [
            shifted(pieces[by], "sec", sections, by) for by in range(1, sections)
        ]

        def gather(*refs):
            out = refs[-1]
            for at, ref in enumerate(refs[:-1]):
                out[:, at * rows : (at + 1) * rows, :] = ref[...]

        (own_memory,) = call(gather, arrived, [((2, group, columns), BF16)], name="gather")
        memories = [own_memory] + [
            shifted(own_memory, "ctx", contexts, by) for by in range(1, contexts)
        ]

        def first_block(starts, query, key, value, gain, grad, store, top, total, weighted, lifted, held):
            context = lax.axis_index("ctx")
            positions = row_positions(starts, context * 4, quarter)
            masks = (
                lambda at: starts[context * 4 + at // quarter] * quarter + at % quarter,
                positions,
            )
            top[...], total[...], weighted[...] = fold_block(
                key, value, query[...], (None, None, None), store, masks, held, scaling
            )
            lifted[...] = (gain[...] * grad[...].astype(F32)).T

        first_store, first_top, first_total, first_weighted, self_lifted = call(
            first_block,
            [block_start, self_query, self_key, self_value, self_gain.reshape(1, columns), self_grad],
            [((frames, frames), BF16), (line, F32), (line, F32), (tall, F32), (tall, F32)],
            flops=2 * frames * unit,
            scratch=[pltpu.VMEM((frames, frames), F32)],
            smem=1,
            name="first_block",
        )

        def statistics(attended, lifted):
            return (
                jnp.sum(attended * attended, axis=0, keepdims=True),
                jnp.sum(lifted * attended, axis=0, keepdims=True),
            )

        def other_blocks(starts, query, top, total, weighted, lifted, *refs):
            keys, values = refs[:others], refs[others : 2 * others]
            stores = refs[2 * others : 3 * others]
            first_weight, weight, attended_ref, stats, held = refs[3 * others :]
            context = lax.axis_index("ctx")
            positions = row_positions(starts, context * 4, quarter)
            running = (top[...], total[...], weighted[...])
            tops = [top[...]]
            for by in range(others):
                source = lax.rem(context - (by + 1) + contexts, contexts)
                masks = (
                    lambda at, source=source: starts[source * 4 + at // quarter] * quarter
                    + at % quarter,
                    positions,
                )
                running = fold_block(
                    keys[by], values[by], query[...], running, stores[by], masks, held, scaling
                )
                tops.append(running[0])
            last = 1.0 / running[1]
            first_weight[...] = jnp.exp(tops[0] - running[0]) * last
            for by in range(others):
                weight[by : by + 1, :] = jnp.exp(tops[by + 1] - running[0]) * last
            attended = running[2] * last
            attended_ref[...] = attended
            stats[0:1, :], stats[1:2, :] = statistics(attended, lifted[...])

        results = call(
            other_blocks,
            [block_start, self_query, first_top, first_total, first_weighted, self_lifted]
            + other_keys
            + other_values,
            [((frames, frames), BF16)] * others
            + [(line, F32), ((others, frames), F32), (tall, F32), ((2, frames), F32)],
            flops=2 * frames * unit * others,
            scratch=[pltpu.VMEM((frames, frames), F32)],
            smem=1,
            name="other_blocks",
        )
        other_stores = results[:others]
        first_weight, other_weight, self_attended, self_stats = results[others:]

        half = frames // 2

        def cross_forward(query, gain, grad, self_stats_ref, *refs):
            blocks, stores = refs[:contexts], refs[contexts : 2 * contexts]
            weight, attended_ref, lifted_ref, stats, packed, held = refs[2 * contexts :]
            running = (None, None, None)
            tops = []
            for at in range(contexts):
                running = fold_block(
                    blocks[at].at[0], blocks[at].at[1], query[...], running, stores[at], None, held, scaling
                )
                tops.append(running[0])
            last = 1.0 / running[1]
            for at in range(contexts):
                weight[at : at + 1, :] = jnp.exp(tops[at] - running[0]) * last
            attended = running[2] * last
            lifted = (gain[...] * grad[...].astype(F32)).T
            attended_ref[...] = attended
            lifted_ref[...] = lifted
            squares, slopes = statistics(attended, lifted)
            stats[0:1, :], stats[1:2, :] = squares, slopes
            lines = [self_stats_ref[0:1, :], self_stats_ref[1:2, :], squares, slopes]
            halves = [entry[:, at : at + half] for entry in lines for at in (0, half)]
            tile = jnp.concatenate(halves, axis=0)
            for at in range(peers):
                packed[at] = tile

        results = call(
            cross_forward,
            [cross_query, cross_gain.reshape(1, columns), cross_grad, self_stats] + memories,
            [((group, frames), BF16)] * contexts
            + [
                ((contexts, frames), F32),
                (tall, F32),
                (tall, F32),
                ((2, frames), F32),
                ((peers, 8, half), F32),
            ],
            flops=2 * group * contexts * unit,
            scratch=[pltpu.VMEM((group, frames), F32)],
            name="cross_forward",
        )
        cross_stores = results[:contexts]
        cross_weight, cross_attended, cross_lifted, cross_stats, packed = results[contexts:]

        received = lax.all_to_all(packed, ("sec", "tp"), split_axis=0, concat_axis=0, tiled=True)

        def norm_terms(received_ref, stats, attended, lifted, at):
            sums = received_ref[0]
            for source in range(1, peers):
                sums = sums + received_ref[source]
            joined = [
                jnp.concatenate([sums[2 * pick : 2 * pick + 1], sums[2 * pick + 1 : 2 * pick + 2]], axis=1)
                for pick in (2 * at, 2 * at + 1)
            ]
            scale = lax.rsqrt(joined[0] / full_width + EPS)
            slope = joined[1] / full_width
            curve = scale * scale * slope
            grad = scale * (lifted[...] - attended[...] * curve)
            delta = scale * (stats[1:2, :] - curve * stats[0:1, :])
            return scale, delta, grad

        def block_grads(key_grad, value_grad, value, store, weight, delta, grad_tall, grad_wide, query, slopes):
            count, step = value.shape[0], 128
            step = min(step, count)
            for at in range(0, count, step):
                products = dot_nn(value[at : at + step, :], grad_tall)
                probs = store[at : at + step, :]
                slope = (probs.astype(F32) * ((products - delta) * weight)).astype(BF16)
                slopes[at : at + step, :] = slope
                key_grad(at, step, dot_nn(slope, query) * scaling)
                value_grad(at, step, dot_nn(probs, grad_wide))

        def cross_backward(received_ref, stats, attended, lifted, weight, query, *refs):
            blocks, stores = refs[:contexts], refs[contexts : 2 * contexts]
            sums, slopes, scale_ref = refs[2 * contexts : 3 * contexts], refs[3 * contexts : 4 * contexts], refs[-1]
            scale, delta, grad = norm_terms(received_ref, stats, attended, lifted, 1)
            scale_ref[...] = scale
            grad_tall = grad.astype(BF16)
            for at in range(contexts):
                line_weight = weight[at : at + 1, :]
                grad_wide = (grad * line_weight).T.astype(BF16)

                def key_grad(first, count, value, out=sums[at]):
                    out[0, first : first + count, :] = value.astype(out.dtype)

                def value_grad(first, count, value, out=sums[at]):
                    out[1, first : first + count, :] = value.astype(out.dtype)

                block_grads(
                    key_grad,
                    value_grad,
                    blocks[at].at[1],
                    stores[at],
                    line_weight,
                    delta,
                    grad_tall,
                    grad_wide,
                    query[...],
                    slopes[at],
                )

        results = call(
            cross_backward,
            [received, cross_stats, cross_attended, cross_lifted, cross_weight, cross_query]
            + memories
            + list(cross_stores),
            [((2, group, columns), F32)]
            + [((2, group, columns), BF16)] * others
            + [((group, frames), BF16)] * contexts
            + [(line, F32)],
            flops=3 * group * contexts * unit,
            name="cross_backward",
        )
        memory_sums, cross_slopes, cross_scale = results[:contexts], results[contexts:-1], results[-1]

        returned = [
            shifted(memory_sums[by], "ctx", contexts, -by) for by in range(1, contexts)
        ]

        def add_up(*refs):
            own, extra, outs = refs[0], refs[1 : 1 + others], refs[1 + others :]
            for at, out in enumerate(outs):
                part = slice(at * rows, (at + 1) * rows)
                total = own[:, part, :]
                for entry in extra:
                    total = total + entry[:, part, :].astype(F32)
                out[...] = total.astype(BF16)

        parts = call(
            add_up, [memory_sums[0]] + returned, [((2, rows, columns), BF16)] * sections, name="add_up"
        )
        back = [parts[0]] + [shifted(parts[by], "sec", sections, -by) for by in range(1, sections)]

        def by_section(*refs):
            out = refs[-1]
            section = lax.axis_index("sec")
            for by, ref in enumerate(refs[:-1]):
                out[lax.rem(section + by, sections)] = ref[...]

        (mine,) = call(by_section, back, [((sections, 2, rows, columns), BF16)], name="by_section")
        lines = [mine] + [shifted(mine, "tp", tensors, by) for by in range(1, tensors)]

        def assemble(*refs):
            sources, key_out, value_out = refs[:tensors], refs[tensors], refs[tensors + 1]
            tensor = lax.axis_index("tp")
            for by, ref in enumerate(sources):
                source = lax.rem(tensor - by + tensors, tensors)
                for section in range(sections):
                    head = section * tensors + source
                    at = pl.ds(pl.multiple_of(head * columns, columns), columns)
                    key_out[:, at] = ref[section, 0]
                    value_out[:, at] = ref[section, 1]

        memory_key_grad, memory_value_grad = call(
            assemble, lines, [(memory_key.shape, BF16), (memory_value.shape, BF16)], name="assemble"
        )

        def other_backward(received_ref, stats, attended, lifted, weight, query, *refs):
            values, stores = refs[:others], refs[others : 2 * others]
            keys_out, values_out = refs[2 * others : 3 * others], refs[3 * others : 4 * others]
            slopes = refs[4 * others : 5 * others]
            grad_ref, scale_ref, delta_ref = refs[5 * others :]
            scale, delta, grad = norm_terms(received_ref, stats, attended, lifted, 0)
            scale_ref[...], delta_ref[...], grad_ref[...] = scale, delta, grad
            grad_tall = grad.astype(BF16)
            for by in range(others):
                line_weight = weight[by : by + 1, :]
                grad_wide = (grad * line_weight).T.astype(BF16)

                def key_grad(first, count, value, out=keys_out[by]):
                    out[first : first + count, :] = value.astype(BF16)

                def value_grad(first, count, value, out=values_out[by]):
                    out[first : first + count, :] = value.astype(BF16)

                block_grads(
                    key_grad,
                    value_grad,
                    values[by],
                    stores[by],
                    line_weight,
                    delta,
                    grad_tall,
                    grad_wide,
                    query[...],
                    slopes[by],
                )

        results = call(
            other_backward,
            [received, self_stats, self_attended, self_lifted, other_weight, self_query]
            + other_values
            + list(other_stores),
            [(wide, BF16)] * (2 * others)
            + [((frames, frames), BF16)] * others
            + [(tall, F32), (line, F32), (line, F32)],
            flops=3 * frames * unit * others,
            name="other_backward",
        )
        away_keys, away_values = results[:others], results[others : 2 * others]
        other_slopes = results[2 * others : 3 * others]
        self_attended_grad, self_scale, self_delta = results[3 * others :]
        home_keys = [shifted(away_keys[by], "ctx", contexts, -(by + 1)) for by in range(others)]
        home_values = [shifted(away_values[by], "ctx", contexts, -(by + 1)) for by in range(others)]

        def own_backward(grad, scale, delta, weight, gain, attended, query, key, value, store, *refs):
            keys, slopes = refs[:others], refs[others : 2 * others]
            key_out, value_out, query_out, out, own_slopes = refs[2 * others :]
            grad_tall = grad[...].astype(BF16)
            line_weight = weight[...]
            grad_wide = (grad[...] * line_weight).T.astype(BF16)

            def key_grad(first, count, result):
                key_out[first : first + count, :] = result

            def value_grad(first, count, result):
                value_out[first : first + count, :] = result

            block_grads(
                key_grad,
                value_grad,
                value,
                store,
                line_weight,
                delta[...],
                grad_tall,
                grad_wide,
                query[...],
                own_slopes,
            )
            total = dot_tn(key[...], own_slopes[...])
            for by in range(others):
                total = total + dot_tn(keys[by][...], slopes[by][...])
            query_out[...] = (total * scaling).T.astype(BF16)
            out[...] = (gain[...] * (attended[...] * scale[...]).T).astype(BF16)

        own_key, own_value, query_grad, self_out = call(
            own_backward,
            [
                self_attended_grad,
                self_scale,
                self_delta,
                first_weight,
                self_gain.reshape(1, columns),
                self_attended,
                self_query,
                self_key,
                self_value,
                first_store,
            ]
            + other_keys
            + list(other_slopes),
            [(wide, F32), (wide, F32), (wide, BF16), (wide, BF16)],
            flops=(4 + others) * frames * unit,
            scratch=[pltpu.VMEM((frames, frames), BF16)],
            name="own_backward",
        )

        def cross_rest(scale, gain, attended, *refs):
            blocks, slopes = refs[:contexts], refs[contexts : 2 * contexts]
            query_out, out = refs[2 * contexts :]
            total = dot_tn(blocks[0][0], slopes[0][...])
            for at in range(1, contexts):
                total = total + dot_tn(blocks[at][0], slopes[at][...])
            query_out[...] = (total * scaling).T.astype(BF16)
            out[...] = (gain[...] * (attended[...] * scale[...]).T).astype(BF16)

        cross_query_grad, cross_out = call(
            cross_rest,
            [cross_scale, cross_gain.reshape(1, columns), cross_attended] + memories + list(cross_slopes),
            [(wide, BF16), (wide, BF16)],
            flops=group * contexts * unit,
            name="cross_rest",
        )

        key_grad = own_key
        value_grad = own_value
        for by in range(others):
            key_grad = key_grad + home_keys[by].astype(F32)
            value_grad = value_grad + home_values[by].astype(F32)
        return (
            self_out,
            cross_out,
            query_grad,
            key_grad.astype(BF16),
            value_grad.astype(BF16),
            cross_query_grad,
            memory_key_grad,
            memory_value_grad,
        )

    rowed = P("ctx", ("sec", "tp"))
    stored = P(("sec", "ctx"), None)
    gains = P(("sec", "tp"))
    return jax.shard_map(
        per_device,
        mesh=mesh,
        in_specs=(rowed, rowed, rowed, gains, rowed, rowed, stored, stored, gains, rowed, P()),
        out_specs=(rowed, rowed, rowed, rowed, rowed, rowed, stored, stored),
        check_vma=False,
    )
```

```python
import math

import jax
import jax.numpy as jnp
from jax import lax
from jax.experimental import pallas as pl
from jax.experimental.pallas import tpu as pltpu
from jax.sharding import PartitionSpec as P


EPS = 1e-06
F32 = jnp.float32
BF16 = jnp.bfloat16
VMEM = pl.BlockSpec(memory_space=pltpu.VMEM)
ROOM = 4 << 20
LIMIT = 60 << 20
SMEM = pl.BlockSpec(memory_space=pltpu.SMEM)
HBM = pl.BlockSpec(memory_space=pltpu.HBM)


def call(body, inputs, outputs, flops=0, scratch=(), smem=0, after=(), loads=False):
    waits = len(after)
    if waits:
        inner, count = body, len(inputs)

        def body(*refs):
            inner(*refs[:count], *refs[count + waits :])

    moved = sum(math.prod(shape) * jnp.dtype(kind).itemsize for shape, kind in outputs)
    moved += sum(entry.size * entry.dtype.itemsize for entry in inputs)
    held = sum(
        math.prod(entry.shape) * jnp.dtype(entry.dtype).itemsize
        for entry in scratch
        if jnp.issubdtype(entry.dtype, jnp.number)
    )
    if loads:
        inputs = [pltpu.with_memory_space_constraint(entry, pltpu.HBM) for entry in inputs]
        shapes = [pltpu.VMEM(shape, kind) for shape, kind in outputs]
    else:
        shapes = [jax.ShapeDtypeStruct(shape, kind) for shape, kind in outputs]
    space = HBM if loads else VMEM
    return list(
        pl.pallas_call(
            body,
            out_shape=shapes,
            in_specs=[SMEM] * smem + [space] * (len(inputs) - smem) + [VMEM] * waits,
            out_specs=[VMEM] * len(outputs),
            scratch_shapes=list(scratch),
            cost_estimate=pl.CostEstimate(flops=flops, bytes_accessed=moved, transcendentals=0),
            compiler_params=pltpu.CompilerParams(
                vmem_limit_bytes=min(2 * (moved + held) + ROOM, LIMIT)
            ),
        )(*inputs, *after)
    )


def dot_nt(left, right):
    return lax.dot_general(left, right, (((1,), (1,)), ((), ())), preferred_element_type=F32)


def dot_nn(left, right):
    return lax.dot_general(left, right, (((1,), (0,)), ((), ())), preferred_element_type=F32)


def dot_tn(left, right):
    return lax.dot_general(left, right, (((0,), (0,)), ((), ())), preferred_element_type=F32)


def row_positions(bases, quarter):
    lanes = lax.broadcasted_iota(jnp.int32, (1, quarter), 1)
    parts = [bases[part : part + 1, part * quarter : (part + 1) * quarter] + lanes for part in range(4)]
    return jnp.concatenate(parts, axis=1)


def fold_block(key, value, queries, running, store, masks, held, scaling):
    rows, step = key.shape[0], 128
    step = min(step, rows)
    top, total, weighted = running
    block_top = top
    for at in range(0, rows, step):
        scores = dot_nt(key[at : at + step, :], queries) * scaling
        if masks is not None:
            key_first, query_positions = masks
            down = lax.broadcasted_iota(jnp.int32, (step, 1), 0)
            scores = jnp.where(down > query_positions - key_first(at), -jnp.inf, scores)
        held[at : at + step, :] = scores
        block_max = jnp.max(scores, axis=0, keepdims=True)
        block_top = block_max if block_top is None else jnp.maximum(block_top, block_max)
    block_total = None
    for at in range(0, rows, step):
        raised = jnp.exp(held[at : at + step, :] - block_top)
        part = jnp.sum(raised, axis=0, keepdims=True)
        block_total = part if block_total is None else block_total + part
        store[at : at + step, :] = raised.astype(BF16)
    product = dot_tn(value[...], store[...])
    if top is None:
        return block_top, block_total, product
    shrink = jnp.exp(top - block_top)
    return block_top, total * shrink + block_total, weighted * shrink + product


def solution(mesh):
    sections, contexts, tensors = mesh.shape["sec"], mesh.shape["ctx"], mesh.shape["tp"]
    peers = sections * tensors

    def shifted(value, axis, count, by):
        return lax.ppermute(value, axis, [(at, (at + by) % count) for at in range(count)])

    def paired(at, by, count):
        return jnp.bitwise_xor(at, by) if count & (count - 1) == 0 else lax.rem(at + by, count)

    def unpaired(at, by, count):
        return jnp.bitwise_xor(at, by) if count & (count - 1) == 0 else lax.rem(at - by + count, count)

    def swapped(value, axis, count, by, back=False):
        if count & (count - 1) == 0:
            return lax.ppermute(value, axis, [(at, at ^ by) for at in range(count)])
        return shifted(value, axis, count, -by if back else by)

    def over_sections(value, by, back=False):
        return swapped(value, "sec", sections, by, back)

    def over_tensors(value, by):
        return swapped(value, "tp", tensors, by)

    def per_device(
        self_query,
        self_key,
        self_value,
        self_gain,
        self_grad,
        cross_query,
        memory_key,
        memory_value,
        cross_gain,
        cross_grad,
        block_start,
    ):
        frames, columns = self_query.shape
        rows = memory_key.shape[0]
        quarter = frames // 4
        full_width = columns * peers
        group = sections * rows
        others = contexts - 1
        scaling = 1.0 / math.sqrt(columns)
        wide = (frames, columns)
        tall = (columns, frames)
        line = (1, frames)
        unit = 2 * frames * columns

        def copy_all(moves, semaphores, meanwhile=None):
            copies = [
                pltpu.make_async_copy(source, target, semaphores.at[at])
                for at, (source, target) in enumerate(moves)
            ]
            for copy in copies:
                copy.start()
            if meanwhile:
                meanwhile()
            for copy in copies:
                copy.wait()

        def load_memory(key_ref, value_ref, *refs):
            outs, semaphores = refs[:-1], refs[-1]
            section, tensor = lax.axis_index("sec"), lax.axis_index("tp")
            moves = []
            for by, out in enumerate(outs):
                head = paired(section, by, sections) * tensors + tensor
                at = pl.ds(pl.multiple_of(head * columns, columns), columns)
                moves += [(key_ref.at[:, at], out.at[0]), (value_ref.at[:, at], out.at[1])]
            copy_all(moves, semaphores)

        pieces = call(
            load_memory,
            [memory_key, memory_value],
            [((2, rows, columns), BF16)] * sections,
            scratch=[pltpu.SemaphoreType.DMA((2 * sections,))],
            loads=True,
        )

        plain = [
            self_query,
            self_key,
            self_value,
            self_grad,
            cross_query,
            cross_grad,
            self_gain.reshape(1, columns),
            cross_gain.reshape(1, columns),
        ]

        def load_rows(starts, *refs):
            count = len(plain)
            bases, semaphores = refs[-2:]

            def positions():
                context = lax.axis_index("ctx")
                for by in range(contexts):
                    source = lax.rem(context - by + contexts, contexts)
                    for part in range(4):
                        at = by * 4 + part
                        first = starts[source * 4 + part] * quarter
                        bases[at : at + 1, :] = jnp.full((1, frames), first, jnp.int32)

            copy_all(list(zip(refs[:count], refs[count : 2 * count])), semaphores, positions)

        other_keys = [shifted(self_key, "ctx", contexts, by) for by in range(1, contexts)]
        other_values = [shifted(self_value, "ctx", contexts, by) for by in range(1, contexts)]

        results = call(
            load_rows,
            [block_start] + plain,
            [(entry.shape, entry.dtype) for entry in plain] + [((4 * contexts, frames), jnp.int32)],
            scratch=[pltpu.SemaphoreType.DMA((len(plain),))],
            smem=1,
            loads=True,
        )
        self_query, self_key, self_value, self_grad, cross_query, cross_grad, self_gain, cross_gain, bases = results

        arrived = [pieces[0]] + [over_sections(pieces[by], by) for by in range(1, sections)]

        def gather(*refs):
            out = refs[-1]
            for at, ref in enumerate(refs[:-1]):
                out[:, at * rows : (at + 1) * rows, :] = ref[...]

        (own_memory,) = call(gather, arrived, [((2, group, columns), BF16)])
        memories = [own_memory] + [
            shifted(own_memory, "ctx", contexts, by) for by in range(1, contexts)
        ]

        def first_block(
            base,
            query,
            key,
            value,
            gain,
            grad,
            cross_gain_ref,
            cross_grad_ref,
            store,
            top,
            total,
            weighted,
            lifted,
            cross_lifted_ref,
            held,
        ):
            masks = (
                lambda at: base[at // quarter : at // quarter + 1, :] + at % quarter,
                row_positions(base, quarter),
            )
            top[...], total[...], weighted[...] = fold_block(
                key, value, query[...], (None, None, None), store, masks, held, scaling
            )
            lifted[...] = (gain[...] * grad[...].astype(F32)).T
            cross_lifted_ref[...] = (cross_gain_ref[...] * cross_grad_ref[...].astype(F32)).T

        first_store, first_top, first_total, first_weighted, self_lifted, cross_lifted = call(
            first_block,
            [
                bases,
                self_query,
                self_key,
                self_value,
                self_gain,
                self_grad,
                cross_gain,
                cross_grad,
            ],
            [((frames, frames), BF16), (line, F32), (line, F32), (tall, F32), (tall, F32), (tall, F32)],
            flops=2 * frames * unit,
            scratch=[pltpu.VMEM((frames, frames), F32)],
        )

        def statistics(attended, lifted):
            return (
                jnp.sum(attended * attended, axis=0, keepdims=True),
                jnp.sum(lifted * attended, axis=0, keepdims=True),
            )

        def other_blocks(base, query, top, total, weighted, lifted, *refs):
            keys, values = refs[:others], refs[others : 2 * others]
            stores = refs[2 * others : 3 * others]
            first_weight, weight, attended_ref, stats, held = refs[3 * others :]
            positions = row_positions(base, quarter)
            running = (top[...], total[...], weighted[...])
            tops = [top[...]]
            for by in range(others):
                first = 4 * (by + 1)
                masks = (
                    lambda at, first=first: base[first + at // quarter : first + at // quarter + 1, :]
                    + at % quarter,
                    positions,
                )
                running = fold_block(
                    keys[by], values[by], query[...], running, stores[by], masks, held, scaling
                )
                tops.append(running[0])
            last = 1.0 / running[1]
            first_weight[...] = jnp.exp(tops[0] - running[0]) * last
            for by in range(others):
                weight[by : by + 1, :] = jnp.exp(tops[by + 1] - running[0]) * last
            attended = running[2] * last
            attended_ref[...] = attended
            stats[0:1, :], stats[1:2, :] = statistics(attended, lifted[...])

        results = call(
            other_blocks,
            [bases, self_query, first_top, first_total, first_weighted, self_lifted]
            + other_keys
            + other_values,
            [((frames, frames), BF16)] * others
            + [(line, F32), ((others, frames), F32), (tall, F32), ((2, frames), F32)],
            flops=2 * frames * unit * others,
            scratch=[pltpu.VMEM((frames, frames), F32)],
        )
        other_stores = results[:others]
        first_weight, other_weight, self_attended, self_stats = results[others:]

        half = frames // 2

        def cross_forward(query, lifted, self_stats_ref, *refs):
            blocks, stores = refs[:contexts], refs[contexts : 2 * contexts]
            weight, attended_ref, stats, packed, held = refs[2 * contexts :]
            running = (None, None, None)
            tops = []
            for at in range(contexts):
                running = fold_block(
                    blocks[at].at[0], blocks[at].at[1], query[...], running, stores[at], None, held, scaling
                )
                tops.append(running[0])
            last = 1.0 / running[1]
            for at in range(contexts):
                weight[at : at + 1, :] = jnp.exp(tops[at] - running[0]) * last
            attended = running[2] * last
            attended_ref[...] = attended
            squares, slopes = statistics(attended, lifted[...])
            stats[0:1, :], stats[1:2, :] = squares, slopes
            lines = [self_stats_ref[0:1, :], self_stats_ref[1:2, :], squares, slopes]
            halves = [entry[:, at : at + half] for entry in lines for at in (0, half)]
            tile = jnp.concatenate(halves, axis=0)
            packed[...] = tile

        results = call(
            cross_forward,
            [cross_query, cross_lifted, self_stats] + memories,
            [((group, frames), BF16)] * contexts
            + [
                ((contexts, frames), F32),
                (tall, F32),
                ((2, frames), F32),
                ((8, half), F32),
            ],
            flops=2 * group * contexts * unit,
            scratch=[pltpu.VMEM((group, frames), F32)],
        )
        cross_stores = results[:contexts]
        cross_weight, cross_attended, cross_stats, packed = results[contexts:]

        def add_all(*refs):
            total = refs[0][...]
            for ref in refs[1:-1]:
                total = total + ref[...]
            refs[-1][...] = total

        near = [packed] + [over_sections(packed, by) for by in range(1, sections)]
        (partial,) = call(add_all, near, [((8, half), F32)])
        received = [partial] + [over_tensors(partial, by) for by in range(1, tensors)]

        def norm_terms(received_ref, stats, attended, lifted, at):
            sums = received_ref[0][...]
            for entry in received_ref[1:]:
                sums = sums + entry[...]
            joined = [
                jnp.concatenate([sums[2 * pick : 2 * pick + 1], sums[2 * pick + 1 : 2 * pick + 2]], axis=1)
                for pick in (2 * at, 2 * at + 1)
            ]
            scale = lax.rsqrt(joined[0] / full_width + EPS)
            slope = joined[1] / full_width
            curve = scale * scale * slope
            grad = scale * (lifted[...] - attended[...] * curve)
            delta = scale * (stats[1:2, :] - curve * stats[0:1, :])
            return scale, delta, grad

        def block_grads(key_grad, value_grad, value, store, weight, delta, grad_tall, grad_wide, query, slopes):
            count, step = value.shape[0], 128
            step = min(step, count)
            for at in range(0, count, step):
                products = dot_nn(value[at : at + step, :], grad_tall)
                probs = store[at : at + step, :]
                slope = (probs.astype(F32) * ((products - delta) * weight)).astype(BF16)
                slopes[at : at + step, :] = slope
                key_grad(at, step, dot_nn(slope, query) * scaling)
                value_grad(at, step, dot_nn(probs, grad_wide))

        def cross_backward(*refs):
            received_ref, (stats, attended, lifted, weight, query) = refs[:tensors], refs[tensors : tensors + 5]
            refs = refs[tensors + 5 :]
            blocks, stores = refs[:contexts], refs[contexts : 2 * contexts]
            sums, slopes, scale_ref = refs[2 * contexts : 3 * contexts], refs[3 * contexts : 4 * contexts], refs[-1]
            scale, delta, grad = norm_terms(received_ref, stats, attended, lifted, 1)
            scale_ref[...] = scale
            grad_tall = grad.astype(BF16)
            for at in range(contexts):
                line_weight = weight[at : at + 1, :]
                grad_wide = (grad * line_weight).T.astype(BF16)

                def key_grad(first, count, value, out=sums[at]):
                    out[0, first : first + count, :] = value.astype(out.dtype)

                def value_grad(first, count, value, out=sums[at]):
                    out[1, first : first + count, :] = value.astype(out.dtype)

                block_grads(
                    key_grad,
                    value_grad,
                    blocks[at].at[1],
                    stores[at],
                    line_weight,
                    delta,
                    grad_tall,
                    grad_wide,
                    query[...],
                    slopes[at],
                )

        results = call(
            cross_backward,
            received
            + [cross_stats, cross_attended, cross_lifted, cross_weight, cross_query]
            + memories
            + list(cross_stores),
            [((2, group, columns), F32)]
            + [((2, group, columns), BF16)] * others
            + [((group, frames), BF16)] * contexts
            + [(line, F32)],
            flops=3 * group * contexts * unit,
        )
        memory_sums, cross_slopes, cross_scale = results[:contexts], results[contexts:-1], results[-1]

        returned = [shifted(memory_sums[by], "ctx", contexts, -by) for by in range(1, contexts)]

        def add_up(*refs):
            own, extra, outs = refs[0], refs[1 : 1 + others], refs[1 + others :]
            for at, out in enumerate(outs):
                part = slice(at * rows, (at + 1) * rows)
                total = own[:, part, :]
                for entry in extra:
                    total = total + entry[:, part, :].astype(F32)
                out[...] = total.astype(BF16)

        parts = call(add_up, [memory_sums[0]] + returned, [((2, rows, columns), BF16)] * sections)
        back = [parts[0]] + [over_sections(parts[by], by, back=True) for by in range(1, sections)]

        def by_section(*refs):
            out = refs[-1]
            section = lax.axis_index("sec")
            for by, ref in enumerate(refs[:-1]):
                out[paired(section, by, sections)] = ref[...]

        (mine,) = call(by_section, back, [((sections, 2, rows, columns), BF16)])
        lines = [mine] + [over_tensors(mine, by) for by in range(1, tensors)]

        def assemble(*refs):
            sources, key_out, value_out = refs[:tensors], refs[tensors], refs[tensors + 1]
            tensor = lax.axis_index("tp")
            for by, ref in enumerate(sources):
                source = unpaired(tensor, by, tensors)
                for section in range(sections):
                    head = section * tensors + source
                    at = pl.ds(pl.multiple_of(head * columns, columns), columns)
                    key_out[:, at] = ref[section, 0]
                    value_out[:, at] = ref[section, 1]

        memory_key_grad, memory_value_grad = call(
            assemble, lines, [(memory_key.shape, BF16), (memory_value.shape, BF16)]
        )

        def other_backward(*refs):
            received_ref, (stats, attended, lifted, weight, query) = refs[:tensors], refs[tensors : tensors + 5]
            refs = refs[tensors + 5 :]
            values, stores = refs[:others], refs[others : 2 * others]
            pairs_out, slopes = refs[2 * others : 3 * others], refs[3 * others : 4 * others]
            grad_ref, scale_ref, delta_ref = refs[4 * others :]
            scale, delta, grad = norm_terms(received_ref, stats, attended, lifted, 0)
            scale_ref[...], delta_ref[...], grad_ref[...] = scale, delta, grad
            grad_tall = grad.astype(BF16)
            for by in range(others):
                line_weight = weight[by : by + 1, :]
                grad_wide = (grad * line_weight).T.astype(BF16)

                def key_grad(first, count, value, out=pairs_out[by]):
                    out[0, first : first + count, :] = value.astype(BF16)

                def value_grad(first, count, value, out=pairs_out[by]):
                    out[1, first : first + count, :] = value.astype(BF16)

                block_grads(
                    key_grad,
                    value_grad,
                    values[by],
                    stores[by],
                    line_weight,
                    delta,
                    grad_tall,
                    grad_wide,
                    query[...],
                    slopes[by],
                )

        results = call(
            other_backward,
            received
            + [self_stats, self_attended, self_lifted, other_weight, self_query]
            + other_values
            + list(other_stores),
            [((2,) + wide, BF16)] * others
            + [((frames, frames), BF16)] * others
            + [(tall, F32), (line, F32), (line, F32)],
            flops=3 * frames * unit * others,
            after=[cross_scale],
        )
        away, other_slopes = results[:others], results[others : 2 * others]
        self_attended_grad, self_scale, self_delta = results[2 * others :]
        home = [shifted(away[by], "ctx", contexts, -(by + 1)) for by in range(others)]

        def own_backward(grad, scale, delta, weight, gain, attended, query, key, value, store, *refs):
            keys, slopes = refs[:others], refs[others : 2 * others]
            key_out, value_out, query_out, out, own_slopes = refs[2 * others :]
            grad_tall = grad[...].astype(BF16)
            line_weight = weight[...]
            grad_wide = (grad[...] * line_weight).T.astype(BF16)

            def key_grad(first, count, result):
                key_out[first : first + count, :] = result

            def value_grad(first, count, result):
                value_out[first : first + count, :] = result

            block_grads(
                key_grad,
                value_grad,
                value,
                store,
                line_weight,
                delta[...],
                grad_tall,
                grad_wide,
                query[...],
                own_slopes,
            )
            total = dot_tn(key[...], own_slopes[...])
            for by in range(others):
                total = total + dot_tn(keys[by][...], slopes[by][...])
            query_out[...] = (total * scaling).T.astype(BF16)
            out[...] = (gain[...] * (attended[...] * scale[...]).T).astype(BF16)

        own_key, own_value, query_grad, self_out = call(
            own_backward,
            [
                self_attended_grad,
                self_scale,
                self_delta,
                first_weight,
                self_gain,
                self_attended,
                self_query,
                self_key,
                self_value,
                first_store,
            ]
            + other_keys
            + list(other_slopes),
            [(wide, F32), (wide, F32), (wide, BF16), (wide, BF16)],
            flops=(4 + others) * frames * unit,
            scratch=[pltpu.VMEM((frames, frames), BF16)],
        )

        def cross_rest(scale, gain, attended, *refs):
            blocks, slopes = refs[:contexts], refs[contexts : 2 * contexts]
            query_out, out = refs[2 * contexts :]
            total = dot_tn(blocks[0][0], slopes[0][...])
            for at in range(1, contexts):
                total = total + dot_tn(blocks[at][0], slopes[at][...])
            query_out[...] = (total * scaling).T.astype(BF16)
            out[...] = (gain[...] * (attended[...] * scale[...]).T).astype(BF16)

        cross_query_grad, cross_out = call(
            cross_rest,
            [cross_scale, cross_gain, cross_attended] + memories + list(cross_slopes),
            [(wide, BF16), (wide, BF16)],
            flops=group * contexts * unit,
        )

        def add_home(own_key_ref, own_value_ref, *refs):
            pairs, key_out, value_out = refs[:others], refs[others], refs[others + 1]
            for at, (own, out) in enumerate(((own_key_ref, key_out), (own_value_ref, value_out))):
                total = own[...]
                for pair in pairs:
                    total = total + pair[at].astype(F32)
                out[...] = total.astype(BF16)

        key_grad, value_grad = call(add_home, [own_key, own_value] + home, [(wide, BF16), (wide, BF16)])
        return (
            self_out,
            cross_out,
            query_grad,
            key_grad,
            value_grad,
            cross_query_grad,
            memory_key_grad,
            memory_value_grad,
        )

    rowed = P("ctx", ("sec", "tp"))
    stored = P(("sec", "ctx"), None)
    gains = P(("sec", "tp"))
    return jax.shard_map(
        per_device,
        mesh=mesh,
        in_specs=(rowed, rowed, rowed, gains, rowed, rowed, stored, stored, gains, rowed, P()),
        out_specs=(rowed, rowed, rowed, rowed, rowed, rowed, stored, stored),
        check_vma=False,
    )
```

```python
import math

import jax
import jax.numpy as jnp
from jax import lax
from jax.experimental import pallas as pl
from jax.experimental.pallas import tpu as pltpu
from jax.sharding import PartitionSpec as P


EPS = 1e-06
F32 = jnp.float32
BF16 = jnp.bfloat16
VMEM = pl.BlockSpec(memory_space=pltpu.VMEM)
ROOM = 4 << 20
LIMIT = 60 << 20
SMEM = pl.BlockSpec(memory_space=pltpu.SMEM)
HBM = pl.BlockSpec(memory_space=pltpu.HBM)


def call(body, inputs, outputs, flops=0, scratch=(), smem=0, after=(), loads=False):
    waits = len(after)
    if waits:
        inner, count = body, len(inputs)

        def body(*refs):
            inner(*refs[:count], *refs[count + waits :])

    moved = sum(math.prod(shape) * jnp.dtype(kind).itemsize for shape, kind in outputs)
    moved += sum(entry.size * entry.dtype.itemsize for entry in inputs)
    held = sum(
        math.prod(entry.shape) * jnp.dtype(entry.dtype).itemsize
        for entry in scratch
        if jnp.issubdtype(entry.dtype, jnp.number)
    )
    if loads:
        inputs = [pltpu.with_memory_space_constraint(entry, pltpu.HBM) for entry in inputs]
        shapes = [pltpu.VMEM(shape, kind) for shape, kind in outputs]
    else:
        shapes = [jax.ShapeDtypeStruct(shape, kind) for shape, kind in outputs]
    space = HBM if loads else VMEM
    return list(
        pl.pallas_call(
            body,
            out_shape=shapes,
            in_specs=[SMEM] * smem + [space] * (len(inputs) - smem) + [VMEM] * waits,
            out_specs=[VMEM] * len(outputs),
            scratch_shapes=list(scratch),
            cost_estimate=pl.CostEstimate(flops=flops, bytes_accessed=moved, transcendentals=0),
            compiler_params=pltpu.CompilerParams(
                vmem_limit_bytes=min(2 * (moved + held) + ROOM, LIMIT)
            ),
        )(*inputs, *after)
    )


def dot_nt(left, right):
    return lax.dot_general(left, right, (((1,), (1,)), ((), ())), preferred_element_type=F32)


def dot_nn(left, right):
    return lax.dot_general(left, right, (((1,), (0,)), ((), ())), preferred_element_type=F32)


def dot_tn(left, right):
    return lax.dot_general(left, right, (((0,), (0,)), ((), ())), preferred_element_type=F32)


def row_positions(bases, quarter):
    lanes = lax.broadcasted_iota(jnp.int32, (1, quarter), 1)
    parts = [bases[part : part + 1, part * quarter : (part + 1) * quarter] + lanes for part in range(4)]
    return jnp.concatenate(parts, axis=1)


def fold_scores(key, queries, running, store, masks, held, scaling):
    rows, step = key.shape[0], 128
    step = min(step, rows)
    top, total = running
    block_top = top
    for at in range(0, rows, step):
        scores = dot_nt(key[at : at + step, :], queries) * scaling
        if masks is not None:
            key_first, query_positions = masks
            down = lax.broadcasted_iota(jnp.int32, (step, 1), 0)
            scores = jnp.where(down > query_positions - key_first(at), -jnp.inf, scores)
        held[at : at + step, :] = scores
        block_max = jnp.max(scores, axis=0, keepdims=True)
        block_top = block_max if block_top is None else jnp.maximum(block_top, block_max)
    block_total = None
    for at in range(0, rows, step):
        raised = jnp.exp(held[at : at + step, :] - block_top)
        part = jnp.sum(raised, axis=0, keepdims=True)
        block_total = part if block_total is None else block_total + part
        store[at : at + step, :] = raised.astype(BF16)
    if top is not None:
        block_total = total * jnp.exp(top - block_top) + block_total
    return block_top, block_total


def solution(mesh):
    sections, contexts, tensors = mesh.shape["sec"], mesh.shape["ctx"], mesh.shape["tp"]
    peers = sections * tensors

    def shifted(value, axis, count, by):
        return lax.ppermute(value, axis, [(at, (at + by) % count) for at in range(count)])

    def paired(at, by, count):
        return jnp.bitwise_xor(at, by) if count & (count - 1) == 0 else lax.rem(at + by, count)

    def unpaired(at, by, count):
        return jnp.bitwise_xor(at, by) if count & (count - 1) == 0 else lax.rem(at - by + count, count)

    def swapped(value, axis, count, by, back=False):
        if count & (count - 1) == 0:
            return lax.ppermute(value, axis, [(at, at ^ by) for at in range(count)])
        return shifted(value, axis, count, -by if back else by)

    def over_sections(value, by, back=False):
        return swapped(value, "sec", sections, by, back)

    def over_tensors(value, by):
        return swapped(value, "tp", tensors, by)


    def per_device(
        self_query,
        self_key,
        self_value,
        self_gain,
        self_grad,
        cross_query,
        memory_key,
        memory_value,
        cross_gain,
        cross_grad,
        block_start,
    ):
        frames, columns = self_query.shape
        rows = memory_key.shape[0]
        quarter = frames // 4
        full_width = columns * peers
        group = sections * rows
        others = contexts - 1
        scaling = 1.0 / math.sqrt(columns)
        wide = (frames, columns)
        tall = (columns, frames)
        line = (1, frames)
        unit = 2 * frames * columns

        def copy_all(moves, semaphores, meanwhile=None):
            copies = [
                pltpu.make_async_copy(source, target, semaphores.at[at])
                for at, (source, target) in enumerate(moves)
            ]
            for copy in copies:
                copy.start()
            if meanwhile:
                meanwhile()
            for copy in copies:
                copy.wait()

        def load_memory(key_ref, value_ref, *refs):
            out, semaphores = refs
            section, tensor = lax.axis_index("sec"), lax.axis_index("tp")
            moves = []
            for by in range(sections):
                head = paired(section, by, sections) * tensors + tensor
                at = pl.ds(pl.multiple_of(head * columns, columns), columns)
                moves += [(key_ref.at[:, at], out.at[by, 0]), (value_ref.at[:, at], out.at[by, 1])]
            copy_all(moves, semaphores)

        (pieces,) = call(
            load_memory,
            [memory_key, memory_value],
            [((sections, 2, rows, columns), BF16)],
            scratch=[pltpu.SemaphoreType.DMA((2 * sections,))],
            loads=True,
        )

        plain = [
            self_query,
            self_key,
            self_value,
            self_grad,
            cross_query,
            cross_grad,
            self_gain.reshape(1, columns),
            cross_gain.reshape(1, columns),
        ]

        def load_rows(start_ref, *refs):
            count = len(plain)
            bases, starts, start_semaphore, semaphores = refs[-4:]
            first_copy = pltpu.make_async_copy(start_ref, starts, start_semaphore)
            first_copy.start()

            def positions():
                first_copy.wait()
                context = lax.axis_index("ctx")
                for by in range(contexts):
                    source = lax.rem(context - by + contexts, contexts)
                    for part in range(4):
                        at = by * 4 + part
                        first = starts[source * 4 + part] * quarter
                        bases[at : at + 1, :] = jnp.full((1, frames), first, jnp.int32)

            copy_all(list(zip(refs[:count], refs[count : 2 * count])), semaphores, positions)

        other_keys = [shifted(self_key, "ctx", contexts, by) for by in range(1, contexts)]
        other_values = [shifted(self_value, "ctx", contexts, by) for by in range(1, contexts)]

        results = call(
            load_rows,
            [block_start] + plain,
            [(entry.shape, entry.dtype) for entry in plain] + [((4 * contexts, frames), jnp.int32)],
            scratch=[
                pltpu.SMEM(block_start.shape, jnp.int32),
                pltpu.SemaphoreType.DMA,
                pltpu.SemaphoreType.DMA((len(plain),)),
            ],
            loads=True,
        )
        self_query, self_key, self_value, self_grad, cross_query, cross_grad, self_gain, cross_gain, bases = results

        blocks_in = [pieces] + [shifted(pieces, "ctx", contexts, by) for by in range(1, contexts)]

        def regroup(*refs):
            ins, outs = refs[:contexts], refs[contexts:]
            for by, out in enumerate(outs):
                for at, ref in enumerate(ins):
                    out[at] = ref[by]

        packs = call(regroup, blocks_in, [((contexts, 2, rows, columns), BF16)] * sections)
        arrived = [packs[0]] + [over_sections(packs[by], by) for by in range(1, sections)]

        def gather(*refs):
            ins, outs = refs[:sections], refs[sections:]
            for at, out in enumerate(outs):
                for by, ref in enumerate(ins):
                    out[:, by * rows : (by + 1) * rows, :] = ref[at]

        memories = call(gather, arrived, [((2, group, columns), BF16)] * contexts)

        def first_block(
            base,
            query,
            key,
            value,
            gain,
            grad,
            cross_gain_ref,
            cross_grad_ref,
            store,
            top,
            total,
            weighted,
            lifted,
            cross_lifted_ref,
            held,
        ):
            masks = (
                lambda at: base[at // quarter : at // quarter + 1, :] + at % quarter,
                row_positions(base, quarter),
            )
            top[...], total[...] = fold_scores(
                key, query[...], (None, None), store, masks, held, scaling
            )
            weighted[...] = dot_tn(value[...], store[...])
            lifted[...] = (gain[...] * grad[...].astype(F32)).T
            cross_lifted_ref[...] = (cross_gain_ref[...] * cross_grad_ref[...].astype(F32)).T

        first_store, first_top, first_total, first_weighted, self_lifted, cross_lifted = call(
            first_block,
            [
                bases,
                self_query,
                self_key,
                self_value,
                self_gain,
                self_grad,
                cross_gain,
                cross_grad,
            ],
            [((frames, frames), BF16), (line, F32), (line, F32), (tall, F32), (tall, F32), (tall, F32)],
            flops=2 * frames * unit,
            scratch=[pltpu.VMEM((frames, frames), F32)],
        )

        def statistics(attended, lifted):
            return (
                jnp.sum(attended * attended, axis=0, keepdims=True),
                jnp.sum(lifted * attended, axis=0, keepdims=True),
            )

        def other_scores(base, query, top, total, *refs):
            keys, stores = refs[:others], refs[others : 2 * others]
            first_weight, weight, held = refs[2 * others :]
            positions = row_positions(base, quarter)
            running = (top[...], total[...])
            tops = [top[...]]
            for by in range(others):
                first = 4 * (by + 1)
                masks = (
                    lambda at, first=first: base[first + at // quarter : first + at // quarter + 1, :]
                    + at % quarter,
                    positions,
                )
                running = fold_scores(keys[by], query[...], running, stores[by], masks, held, scaling)
                tops.append(running[0])
            last = 1.0 / running[1]
            first_weight[...] = jnp.exp(tops[0] - running[0]) * last
            for by in range(others):
                weight[by : by + 1, :] = jnp.exp(tops[by + 1] - running[0]) * last

        results = call(
            other_scores,
            [bases, self_query, first_top, first_total] + other_keys,
            [((frames, frames), BF16)] * others + [(line, F32), ((others, frames), F32)],
            flops=frames * unit * others,
            scratch=[pltpu.VMEM((frames, frames), F32)],
        )
        other_stores, (first_weight, other_weight) = results[:others], results[others:]

        def cross_forward(query, lifted, *refs):
            blocks, stores = refs[:contexts], refs[contexts : 2 * contexts]
            weight, attended_ref, stats, held = refs[2 * contexts :]
            running = (None, None)
            tops = []
            for at in range(contexts):
                running = fold_scores(blocks[at].at[0], query[...], running, stores[at], None, held, scaling)
                tops.append(running[0])
            last = 1.0 / running[1]
            attended = None
            for at in range(contexts):
                factor = jnp.exp(tops[at] - running[0]) * last
                weight[at : at + 1, :] = factor
                part = dot_tn(blocks[at][1], stores[at][...]) * factor
                attended = part if attended is None else attended + part
            attended_ref[...] = attended
            stats[0:1, :], stats[1:2, :] = statistics(attended, lifted[...])

        results = call(
            cross_forward,
            [cross_query, cross_lifted] + memories,
            [((group, frames), BF16)] * contexts
            + [
                ((contexts, frames), F32),
                (tall, F32),
                ((2, frames), F32),
            ],
            flops=2 * group * contexts * unit,
            scratch=[pltpu.VMEM((group, frames), F32)],
        )
        cross_stores = results[:contexts]
        cross_weight, cross_attended, cross_stats = results[contexts:]

        half = frames // 2

        def other_values_seen(weighted, first_weight_ref, weight, lifted, cross_stats_ref, *refs):
            values, stores = refs[:others], refs[others : 2 * others]
            attended_ref, stats, packed = refs[2 * others :]
            attended = weighted[...] * first_weight_ref[...]
            for by in range(others):
                attended = attended + dot_tn(values[by][...], stores[by][...]) * weight[by : by + 1, :]
            attended_ref[...] = attended
            squares, slopes = statistics(attended, lifted[...])
            stats[0:1, :], stats[1:2, :] = squares, slopes
            lines = [squares, slopes, cross_stats_ref[0:1, :], cross_stats_ref[1:2, :]]
            halves = [entry[:, at : at + half] for entry in lines for at in (0, half)]
            tile = jnp.concatenate(halves, axis=0)
            for at in range(peers):
                packed[at] = tile

        self_attended, self_stats, packed = call(
            other_values_seen,
            [first_weighted, first_weight, other_weight, self_lifted, cross_stats] + other_values + other_stores,
            [(tall, F32), ((2, frames), F32), ((peers, 8, half), F32)],
            flops=frames * unit * others,
        )


        received = [lax.all_to_all(packed, ("sec", "tp"), split_axis=0, concat_axis=0, tiled=True)]

        def norm_terms(received_ref, stats, attended, lifted, at):
            sums = received_ref[0][0]
            for source in range(1, peers):
                sums = sums + received_ref[0][source]
            joined = [
                jnp.concatenate([sums[2 * pick : 2 * pick + 1], sums[2 * pick + 1 : 2 * pick + 2]], axis=1)
                for pick in (2 * at, 2 * at + 1)
            ]
            scale = lax.rsqrt(joined[0] / full_width + EPS)
            slope = joined[1] / full_width
            curve = scale * scale * slope
            grad = scale * (lifted[...] - attended[...] * curve)
            delta = scale * (stats[1:2, :] - curve * stats[0:1, :])
            return scale, delta, grad

        def block_grads(key_grad, value_grad, value, store, weight, delta, grad_tall, grad_wide, query, slopes):
            count, step = value.shape[0], 128
            step = min(step, count)
            for at in range(0, count, step):
                products = dot_nn(value[at : at + step, :], grad_tall)
                probs = store[at : at + step, :]
                slope = (probs.astype(F32) * ((products - delta) * weight)).astype(BF16)
                slopes[at : at + step, :] = slope
                key_grad(at, step, dot_nn(slope, query) * scaling)
                value_grad(at, step, dot_nn(probs, grad_wide))

        def memory_grads(block, store, factor, delta, grad, query, out, slopes):
            grad_wide = (grad * factor).T.astype(BF16)

            def key_grad(first, count, value):
                out[0, first : first + count, :] = value.astype(out.dtype)

            def value_grad(first, count, value):
                out[1, first : first + count, :] = value.astype(out.dtype)

            block_grads(
                key_grad,
                value_grad,
                block.at[1],
                store,
                factor,
                delta,
                grad.astype(BF16),
                grad_wide,
                query[...],
                slopes,
            )

        def cross_backward(*refs):
            received_ref, (stats, attended, lifted, weight, query) = refs[:1], refs[1:6]
            refs = refs[6:]
            blocks, stores = refs[:others], refs[others : 2 * others]
            sums, slopes = refs[2 * others : 3 * others], refs[3 * others : 4 * others]
            scale_ref, delta_ref, grad_ref = refs[4 * others :]
            scale, delta, grad = norm_terms(received_ref, stats, attended, lifted, 1)
            scale_ref[...], delta_ref[...], grad_ref[...] = scale, delta, grad
            for by in range(others):
                factor = weight[by + 1 : by + 2, :]
                memory_grads(blocks[by], stores[by], factor, delta, grad, query, sums[by], slopes[by])

        results = call(
            cross_backward,
            received
            + [cross_stats, cross_attended, cross_lifted, cross_weight, cross_query]
            + memories[1:]
            + cross_stores[1:],
            [((2, group, columns), BF16)] * others
            + [((group, frames), BF16)] * others
            + [(line, F32), (line, F32), (tall, F32)],
            flops=3 * group * others * unit,
        )
        away_sums, away_slopes = results[:others], results[others : 2 * others]
        cross_scale, cross_delta, cross_attended_grad = results[2 * others :]

        def cross_own(delta, grad, weight, query, block, store, out, slopes):
            memory_grads(block, store, weight[0:1, :], delta[...], grad[...], query, out, slopes)

        own_sums, own_slopes_cross = call(
            cross_own,
            [cross_delta, cross_attended_grad, cross_weight, cross_query, memories[0], cross_stores[0]],
            [((2, group, columns), F32), ((group, frames), BF16)],
            flops=3 * group * unit,
        )
        cross_slopes = [own_slopes_cross] + away_slopes

        returned = [shifted(away_sums[by], "ctx", contexts, -(by + 1)) for by in range(others)]

        def add_up(*refs):
            own, extra, outs = refs[0], refs[1 : 1 + others], refs[1 + others :]
            for at, out in enumerate(outs):
                part = slice(at * rows, (at + 1) * rows)
                total = own[:, part, :]
                for entry in extra:
                    total = total + entry[:, part, :].astype(F32)
                out[...] = total.astype(BF16)

        parts = call(add_up, [own_sums] + returned, [((2, rows, columns), BF16)] * sections)
        back = [parts[0]] + [over_sections(parts[by], by, back=True) for by in range(1, sections)]

        def by_section(*refs):
            out = refs[-1]
            section = lax.axis_index("sec")
            for by, ref in enumerate(refs[:-1]):
                out[paired(section, by, sections)] = ref[...]

        (mine,) = call(by_section, back, [((sections, 2, rows, columns), BF16)])
        lines = [mine] + [over_tensors(mine, by) for by in range(1, tensors)]

        def assemble(*refs):
            sources, key_out, value_out = refs[:tensors], refs[tensors], refs[tensors + 1]
            tensor = lax.axis_index("tp")
            for by, ref in enumerate(sources):
                source = unpaired(tensor, by, tensors)
                for section in range(sections):
                    head = section * tensors + source
                    at = pl.ds(pl.multiple_of(head * columns, columns), columns)
                    key_out[:, at] = ref[section, 0]
                    value_out[:, at] = ref[section, 1]

        memory_key_grad, memory_value_grad = call(
            assemble, lines, [(memory_key.shape, BF16), (memory_value.shape, BF16)]
        )

        def other_backward(*refs):
            received_ref, (stats, attended, lifted, weight, query) = refs[:1], refs[1:6]
            refs = refs[6:]
            values, stores = refs[:others], refs[others : 2 * others]
            pairs_out, slopes = refs[2 * others : 3 * others], refs[3 * others : 4 * others]
            grad_ref, scale_ref, delta_ref = refs[4 * others :]
            scale, delta, grad = norm_terms(received_ref, stats, attended, lifted, 0)
            scale_ref[...], delta_ref[...], grad_ref[...] = scale, delta, grad
            grad_tall = grad.astype(BF16)
            for by in range(others):
                line_weight = weight[by : by + 1, :]
                grad_wide = (grad * line_weight).T.astype(BF16)

                def key_grad(first, count, value, out=pairs_out[by]):
                    out[0, first : first + count, :] = value.astype(BF16)

                def value_grad(first, count, value, out=pairs_out[by]):
                    out[1, first : first + count, :] = value.astype(BF16)

                block_grads(
                    key_grad,
                    value_grad,
                    values[by],
                    stores[by],
                    line_weight,
                    delta,
                    grad_tall,
                    grad_wide,
                    query[...],
                    slopes[by],
                )

        results = call(
            other_backward,
            received
            + [self_stats, self_attended, self_lifted, other_weight, self_query]
            + other_values
            + list(other_stores),
            [((2,) + wide, BF16)] * others
            + [((frames, frames), BF16)] * others
            + [(tall, F32), (line, F32), (line, F32)],
            flops=3 * frames * unit * others,
            after=[cross_scale],
        )
        away, other_slopes = results[:others], results[others : 2 * others]
        self_attended_grad, self_scale, self_delta = results[2 * others :]
        home = [shifted(away[by], "ctx", contexts, -(by + 1)) for by in range(others)]

        def own_backward(grad, scale, delta, weight, gain, attended, query, key, value, store, *refs):
            keys, slopes = refs[:others], refs[others : 2 * others]
            key_out, value_out, query_out, out, own_slopes = refs[2 * others :]
            grad_tall = grad[...].astype(BF16)
            line_weight = weight[...]
            grad_wide = (grad[...] * line_weight).T.astype(BF16)

            def key_grad(first, count, result):
                key_out[first : first + count, :] = result

            def value_grad(first, count, result):
                value_out[first : first + count, :] = result

            block_grads(
                key_grad,
                value_grad,
                value,
                store,
                line_weight,
                delta[...],
                grad_tall,
                grad_wide,
                query[...],
                own_slopes,
            )
            total = dot_tn(key[...], own_slopes[...])
            for by in range(others):
                total = total + dot_tn(keys[by][...], slopes[by][...])
            query_out[...] = (total * scaling).T.astype(BF16)
            out[...] = (gain[...] * (attended[...] * scale[...]).T).astype(BF16)

        own_key, own_value, query_grad, self_out = call(
            own_backward,
            [
                self_attended_grad,
                self_scale,
                self_delta,
                first_weight,
                self_gain,
                self_attended,
                self_query,
                self_key,
                self_value,
                first_store,
            ]
            + other_keys
            + list(other_slopes),
            [(wide, F32), (wide, F32), (wide, BF16), (wide, BF16)],
            flops=(4 + others) * frames * unit,
            scratch=[pltpu.VMEM((frames, frames), BF16)],
        )

        def cross_rest(scale, gain, attended, *refs):
            blocks, slopes = refs[:contexts], refs[contexts : 2 * contexts]
            query_out, out = refs[2 * contexts :]
            total = dot_tn(blocks[0][0], slopes[0][...])
            for at in range(1, contexts):
                total = total + dot_tn(blocks[at][0], slopes[at][...])
            query_out[...] = (total * scaling).T.astype(BF16)
            out[...] = (gain[...] * (attended[...] * scale[...]).T).astype(BF16)

        cross_query_grad, cross_out = call(
            cross_rest,
            [cross_scale, cross_gain, cross_attended] + memories + list(cross_slopes),
            [(wide, BF16), (wide, BF16)],
            flops=group * contexts * unit,
        )

        def add_home(own_key_ref, own_value_ref, *refs):
            pairs, key_out, value_out = refs[:others], refs[others], refs[others + 1]
            for at, (own, out) in enumerate(((own_key_ref, key_out), (own_value_ref, value_out))):
                total = own[...]
                for pair in pairs:
                    total = total + pair[at].astype(F32)
                out[...] = total.astype(BF16)

        key_grad, value_grad = call(add_home, [own_key, own_value] + home, [(wide, BF16), (wide, BF16)])
        return (
            self_out,
            cross_out,
            query_grad,
            key_grad,
            value_grad,
            cross_query_grad,
            memory_key_grad,
            memory_value_grad,
        )

    rowed = P("ctx", ("sec", "tp"))
    stored = P(("sec", "ctx"), None)
    gains = P(("sec", "tp"))
    return jax.shard_map(
        per_device,
        mesh=mesh,
        in_specs=(rowed, rowed, rowed, gains, rowed, rowed, stored, stored, gains, rowed, P()),
        out_specs=(rowed, rowed, rowed, rowed, rowed, rowed, stored, stored),
        check_vma=False,
    )
```

```python
import math

import jax
import jax.numpy as jnp
from jax import lax
from jax.experimental import pallas as pl
from jax.experimental.pallas import tpu as pltpu
from jax.sharding import PartitionSpec as P


EPS = 1e-06
F32 = jnp.float32
BF16 = jnp.bfloat16
VMEM = pl.BlockSpec(memory_space=pltpu.VMEM)
ROOM = 4 << 20
LIMIT = 60 << 20
SMEM = pl.BlockSpec(memory_space=pltpu.SMEM)
HBM = pl.BlockSpec(memory_space=pltpu.HBM)


def call(body, inputs, outputs, flops=0, scratch=(), smem=0, after=(), loads=False):
    waits = len(after)
    if waits:
        inner, count = body, len(inputs)

        def body(*refs):
            inner(*refs[:count], *refs[count + waits :])

    moved = sum(math.prod(shape) * jnp.dtype(kind).itemsize for shape, kind in outputs)
    moved += sum(entry.size * entry.dtype.itemsize for entry in inputs)
    held = sum(
        math.prod(entry.shape) * jnp.dtype(entry.dtype).itemsize
        for entry in scratch
        if jnp.issubdtype(entry.dtype, jnp.number)
    )
    if loads:
        inputs = [pltpu.with_memory_space_constraint(entry, pltpu.HBM) for entry in inputs]
        shapes = [pltpu.VMEM(shape, kind) for shape, kind in outputs]
    else:
        shapes = [jax.ShapeDtypeStruct(shape, kind) for shape, kind in outputs]
    space = HBM if loads else VMEM
    return list(
        pl.pallas_call(
            body,
            out_shape=shapes,
            in_specs=[SMEM] * smem + [space] * (len(inputs) - smem) + [VMEM] * waits,
            out_specs=[VMEM] * len(outputs),
            scratch_shapes=list(scratch),
            cost_estimate=pl.CostEstimate(flops=flops, bytes_accessed=moved, transcendentals=0),
            compiler_params=pltpu.CompilerParams(
                vmem_limit_bytes=min(2 * (moved + held) + ROOM, LIMIT)
            ),
        )(*inputs, *after)
    )


def dot_nt(left, right):
    return lax.dot_general(left, right, (((1,), (1,)), ((), ())), preferred_element_type=F32)


def dot_nn(left, right):
    return lax.dot_general(left, right, (((1,), (0,)), ((), ())), preferred_element_type=F32)


def dot_tn(left, right):
    return lax.dot_general(left, right, (((0,), (0,)), ((), ())), preferred_element_type=F32)


def row_positions(bases, quarter):
    lanes = lax.broadcasted_iota(jnp.int32, (1, quarter), 1)
    parts = [bases[part : part + 1, part * quarter : (part + 1) * quarter] + lanes for part in range(4)]
    return jnp.concatenate(parts, axis=1)


def fold_scores(key, queries, running, store, masks, held, scaling):
    rows, step = key.shape[0], 128
    step = min(step, rows)
    top, total = running
    block_top = top
    for at in range(0, rows, step):
        scores = dot_nt(key[at : at + step, :], queries) * scaling
        if masks is not None:
            key_first, query_positions = masks
            down = lax.broadcasted_iota(jnp.int32, (step, 1), 0)
            scores = jnp.where(down > query_positions - key_first(at), -jnp.inf, scores)
        held[at : at + step, :] = scores
        block_max = jnp.max(scores, axis=0, keepdims=True)
        block_top = block_max if block_top is None else jnp.maximum(block_top, block_max)
    block_total = None
    for at in range(0, rows, step):
        raised = jnp.exp(held[at : at + step, :] - block_top)
        part = jnp.sum(raised, axis=0, keepdims=True)
        block_total = part if block_total is None else block_total + part
        store[at : at + step, :] = raised.astype(BF16)
    if top is not None:
        block_total = total * jnp.exp(top - block_top) + block_total
    return block_top, block_total


def solution(mesh):
    sections, contexts, tensors = mesh.shape["sec"], mesh.shape["ctx"], mesh.shape["tp"]
    peers = sections * tensors

    def shifted(value, axis, count, by):
        return lax.ppermute(value, axis, [(at, (at + by) % count) for at in range(count)])

    def paired(at, by, count):
        return jnp.bitwise_xor(at, by) if count & (count - 1) == 0 else lax.rem(at + by, count)

    def unpaired(at, by, count):
        return jnp.bitwise_xor(at, by) if count & (count - 1) == 0 else lax.rem(at - by + count, count)

    def swapped(value, axis, count, by, back=False):
        if count & (count - 1) == 0:
            return lax.ppermute(value, axis, [(at, at ^ by) for at in range(count)])
        return shifted(value, axis, count, -by if back else by)

    def over_sections(value, by, back=False):
        return swapped(value, "sec", sections, by, back)

    def over_tensors(value, by):
        return swapped(value, "tp", tensors, by)


    def per_device(
        self_query,
        self_key,
        self_value,
        self_gain,
        self_grad,
        cross_query,
        memory_key,
        memory_value,
        cross_gain,
        cross_grad,
        block_start,
    ):
        frames, columns = self_query.shape
        rows = memory_key.shape[0]
        quarter = frames // 4
        full_width = columns * peers
        group = sections * rows
        others = contexts - 1
        scaling = 1.0 / math.sqrt(columns)
        wide = (frames, columns)
        tall = (columns, frames)
        line = (1, frames)
        unit = 2 * frames * columns

        def copy_all(moves, semaphores, meanwhile=None):
            copies = [
                pltpu.make_async_copy(source, target, semaphores.at[at])
                for at, (source, target) in enumerate(moves)
            ]
            for copy in copies:
                copy.start()
            if meanwhile:
                meanwhile()
            for copy in copies:
                copy.wait()

        def load_memory(key_ref, value_ref, *refs):
            out, semaphores = refs
            section, tensor = lax.axis_index("sec"), lax.axis_index("tp")
            moves = []
            for by in range(sections):
                head = paired(section, by, sections) * tensors + tensor
                at = pl.ds(pl.multiple_of(head * columns, columns), columns)
                moves += [(key_ref.at[:, at], out.at[by, 0]), (value_ref.at[:, at], out.at[by, 1])]
            copy_all(moves, semaphores)

        (pieces,) = call(
            load_memory,
            [memory_key, memory_value],
            [((sections, 2, rows, columns), BF16)],
            scratch=[pltpu.SemaphoreType.DMA((2 * sections,))],
            loads=True,
        )

        plain = [
            self_query,
            self_key,
            self_value,
            self_grad,
            cross_query,
            cross_grad,
            self_gain.reshape(1, columns),
            cross_gain.reshape(1, columns),
        ]

        def load_rows(start_ref, *refs):
            count = len(plain)
            bases, starts, start_semaphore, semaphores = refs[-4:]
            first_copy = pltpu.make_async_copy(start_ref, starts, start_semaphore)
            first_copy.start()

            def positions():
                first_copy.wait()
                context = lax.axis_index("ctx")
                for by in range(contexts):
                    source = lax.rem(context - by + contexts, contexts)
                    for part in range(4):
                        at = by * 4 + part
                        first = starts[source * 4 + part] * quarter
                        bases[at : at + 1, :] = jnp.full((1, frames), first, jnp.int32)

            copy_all(list(zip(refs[:count], refs[count : 2 * count])), semaphores, positions)

        other_keys = [shifted(self_key, "ctx", contexts, by) for by in range(1, contexts)]
        other_values = [shifted(self_value, "ctx", contexts, by) for by in range(1, contexts)]

        results = call(
            load_rows,
            [block_start] + plain,
            [(entry.shape, entry.dtype) for entry in plain] + [((4 * contexts, frames), jnp.int32)],
            scratch=[
                pltpu.SMEM(block_start.shape, jnp.int32),
                pltpu.SemaphoreType.DMA,
                pltpu.SemaphoreType.DMA((len(plain),)),
            ],
            loads=True,
        )
        self_query, self_key, self_value, self_grad, cross_query, cross_grad, self_gain, cross_gain, bases = results

        blocks_in = [pieces] + [shifted(pieces, "ctx", contexts, by) for by in range(1, contexts)]

        def regroup(*refs):
            ins, outs = refs[:contexts], refs[contexts:]
            for by, out in enumerate(outs):
                for at, ref in enumerate(ins):
                    out[at] = ref[by]

        packs = call(regroup, blocks_in, [((contexts, 2, rows, columns), BF16)] * sections)
        arrived = [packs[0]] + [over_sections(packs[by], by) for by in range(1, sections)]

        def gather(*refs):
            ins, outs = refs[:sections], refs[sections:]
            for at, out in enumerate(outs):
                for by, ref in enumerate(ins):
                    out[:, by * rows : (by + 1) * rows, :] = ref[at]

        memories = call(gather, arrived, [((2, group, columns), BF16)] * contexts)

        def first_block(
            base,
            query,
            key,
            value,
            gain,
            grad,
            cross_gain_ref,
            cross_grad_ref,
            store,
            top,
            total,
            weighted,
            lifted,
            cross_lifted_ref,
            held,
        ):
            masks = (
                lambda at: base[at // quarter : at // quarter + 1, :] + at % quarter,
                row_positions(base, quarter),
            )
            top[...], total[...] = fold_scores(
                key, query[...], (None, None), store, masks, held, scaling
            )
            weighted[...] = dot_tn(value[...], store[...])
            lifted[...] = (gain[...] * grad[...].astype(F32)).T
            cross_lifted_ref[...] = (cross_gain_ref[...] * cross_grad_ref[...].astype(F32)).T

        first_store, first_top, first_total, first_weighted, self_lifted, cross_lifted = call(
            first_block,
            [
                bases,
                self_query,
                self_key,
                self_value,
                self_gain,
                self_grad,
                cross_gain,
                cross_grad,
            ],
            [((frames, frames), BF16), (line, F32), (line, F32), (tall, F32), (tall, F32), (tall, F32)],
            flops=2 * frames * unit,
            scratch=[pltpu.VMEM((frames, frames), F32)],
        )

        def statistics(attended, lifted):
            return (
                jnp.sum(attended * attended, axis=0, keepdims=True),
                jnp.sum(lifted * attended, axis=0, keepdims=True),
            )

        def other_scores(base, query, top, total, *refs):
            keys, stores = refs[:others], refs[others : 2 * others]
            first_weight, weight, held = refs[2 * others :]
            positions = row_positions(base, quarter)
            running = (top[...], total[...])
            tops = [top[...]]
            for by in range(others):
                first = 4 * (by + 1)
                masks = (
                    lambda at, first=first: base[first + at // quarter : first + at // quarter + 1, :]
                    + at % quarter,
                    positions,
                )
                running = fold_scores(keys[by], query[...], running, stores[by], masks, held, scaling)
                tops.append(running[0])
            last = 1.0 / running[1]
            first_weight[...] = jnp.exp(tops[0] - running[0]) * last
            for by in range(others):
                weight[by : by + 1, :] = jnp.exp(tops[by + 1] - running[0]) * last

        results = call(
            other_scores,
            [bases, self_query, first_top, first_total] + other_keys,
            [((frames, frames), BF16)] * others + [(line, F32), ((others, frames), F32)],
            flops=frames * unit * others,
            scratch=[pltpu.VMEM((frames, frames), F32)],
        )
        other_stores, (first_weight, other_weight) = results[:others], results[others:]

        def cross_forward(query, lifted, *refs):
            blocks, stores = refs[:contexts], refs[contexts : 2 * contexts]
            weight, attended_ref, stats, held = refs[2 * contexts :]
            running = (None, None)
            tops = []
            for at in range(contexts):
                running = fold_scores(blocks[at].at[0], query[...], running, stores[at], None, held, scaling)
                tops.append(running[0])
            last = 1.0 / running[1]
            attended = None
            for at in range(contexts):
                factor = jnp.exp(tops[at] - running[0]) * last
                weight[at : at + 1, :] = factor
                part = dot_tn(blocks[at][1], stores[at][...]) * factor
                attended = part if attended is None else attended + part
            attended_ref[...] = attended
            stats[0:1, :], stats[1:2, :] = statistics(attended, lifted[...])

        results = call(
            cross_forward,
            [cross_query, cross_lifted] + memories,
            [((group, frames), BF16)] * contexts
            + [
                ((contexts, frames), F32),
                (tall, F32),
                ((2, frames), F32),
            ],
            flops=2 * group * contexts * unit,
            scratch=[pltpu.VMEM((group, frames), F32)],
        )
        cross_stores = results[:contexts]
        cross_weight, cross_attended, cross_stats = results[contexts:]

        half = frames // 2

        def other_values_seen(weighted, first_weight_ref, weight, lifted, cross_stats_ref, *refs):
            values, stores = refs[:others], refs[others : 2 * others]
            attended_ref, stats, packed = refs[2 * others :]
            attended = weighted[...] * first_weight_ref[...]
            for by in range(others):
                attended = attended + dot_tn(values[by][...], stores[by][...]) * weight[by : by + 1, :]
            attended_ref[...] = attended
            squares, slopes = statistics(attended, lifted[...])
            stats[0:1, :], stats[1:2, :] = squares, slopes
            lines = [squares, slopes, cross_stats_ref[0:1, :], cross_stats_ref[1:2, :]]
            halves = [entry[:, at : at + half] for entry in lines for at in (0, half)]
            tile = jnp.concatenate(halves, axis=0)
            for at in range(peers):
                packed[at] = tile.astype(BF16)

        self_attended, self_stats, packed = call(
            other_values_seen,
            [first_weighted, first_weight, other_weight, self_lifted, cross_stats] + other_values + other_stores,
            [(tall, F32), ((2, frames), F32), ((peers, 8, half), BF16)],
            flops=frames * unit * others,
        )


        received = [lax.all_to_all(packed, ("sec", "tp"), split_axis=0, concat_axis=0, tiled=True)]

        def norm_terms(received_ref, stats, attended, lifted, at):
            sums = received_ref[0][0].astype(F32)
            for source in range(1, peers):
                sums = sums + received_ref[0][source].astype(F32)
            joined = [
                jnp.concatenate([sums[2 * pick : 2 * pick + 1], sums[2 * pick + 1 : 2 * pick + 2]], axis=1)
                for pick in (2 * at, 2 * at + 1)
            ]
            scale = lax.rsqrt(joined[0] / full_width + EPS)
            slope = joined[1] / full_width
            curve = scale * scale * slope
            grad = scale * (lifted[...] - attended[...] * curve)
            delta = scale * (stats[1:2, :] - curve * stats[0:1, :])
            return scale, delta, grad

        def block_grads(key_grad, value_grad, value, store, weight, delta, grad_tall, grad_folded, query, slopes):
            count, step = value.shape[0], 128
            step = min(step, count)
            for at in range(0, count, step):
                products = dot_nn(value[at : at + step, :], grad_tall)
                probs = store[at : at + step, :]
                slope = (probs.astype(F32) * ((products - delta) * weight)).astype(BF16)
                slopes[at : at + step, :] = slope
                key_grad(at, step, dot_nn(slope, query) * scaling)
                value_grad(at, step, dot_nt(probs, grad_folded))

        def memory_grads(block, store, factor, delta, grad, query, out, slopes):
            grad_folded = (grad * factor).astype(BF16)

            def key_grad(first, count, value):
                out[0, first : first + count, :] = value.astype(out.dtype)

            def value_grad(first, count, value):
                out[1, first : first + count, :] = value.astype(out.dtype)

            block_grads(
                key_grad,
                value_grad,
                block.at[1],
                store,
                factor,
                delta,
                grad.astype(BF16),
                grad_folded,
                query[...],
                slopes,
            )

        def cross_backward(*refs):
            received_ref, (stats, attended, lifted, weight, query) = refs[:1], refs[1:6]
            refs = refs[6:]
            blocks, stores = refs[:others], refs[others : 2 * others]
            sums, slopes = refs[2 * others : 3 * others], refs[3 * others : 4 * others]
            scale_ref, delta_ref, grad_ref = refs[4 * others :]
            scale, delta, grad = norm_terms(received_ref, stats, attended, lifted, 1)
            scale_ref[...], delta_ref[...], grad_ref[...] = scale, delta, grad
            for by in range(others):
                factor = weight[by + 1 : by + 2, :]
                memory_grads(blocks[by], stores[by], factor, delta, grad, query, sums[by], slopes[by])

        results = call(
            cross_backward,
            received
            + [cross_stats, cross_attended, cross_lifted, cross_weight, cross_query]
            + memories[1:]
            + cross_stores[1:],
            [((2, group, columns), BF16)] * others
            + [((group, frames), BF16)] * others
            + [(line, F32), (line, F32), (tall, F32)],
            flops=3 * group * others * unit,
        )
        away_sums, away_slopes = results[:others], results[others : 2 * others]
        cross_scale, cross_delta, cross_attended_grad = results[2 * others :]

        def cross_own(delta, grad, weight, query, block, store, out, slopes):
            memory_grads(block, store, weight[0:1, :], delta[...], grad[...], query, out, slopes)

        own_sums, own_slopes_cross = call(
            cross_own,
            [cross_delta, cross_attended_grad, cross_weight, cross_query, memories[0], cross_stores[0]],
            [((2, group, columns), F32), ((group, frames), BF16)],
            flops=3 * group * unit,
        )
        cross_slopes = [own_slopes_cross] + away_slopes

        returned = [shifted(away_sums[by], "ctx", contexts, -(by + 1)) for by in range(others)]

        def add_up(*refs):
            own, extra, outs = refs[0], refs[1 : 1 + others], refs[1 + others :]
            for at, out in enumerate(outs):
                part = slice(at * rows, (at + 1) * rows)
                total = own[:, part, :]
                for entry in extra:
                    total = total + entry[:, part, :].astype(F32)
                out[...] = total.astype(BF16)

        parts = call(add_up, [own_sums] + returned, [((2, rows, columns), BF16)] * sections)
        back = [parts[0]] + [over_sections(parts[by], by, back=True) for by in range(1, sections)]

        def by_section(*refs):
            out = refs[-1]
            section = lax.axis_index("sec")
            for by, ref in enumerate(refs[:-1]):
                out[paired(section, by, sections)] = ref[...]

        (mine,) = call(by_section, back, [((sections, 2, rows, columns), BF16)])
        lines = [mine] + [over_tensors(mine, by) for by in range(1, tensors)]

        def assemble(*refs):
            sources, key_out, value_out = refs[:tensors], refs[tensors], refs[tensors + 1]
            tensor = lax.axis_index("tp")
            for by, ref in enumerate(sources):
                source = unpaired(tensor, by, tensors)
                for section in range(sections):
                    head = section * tensors + source
                    at = pl.ds(pl.multiple_of(head * columns, columns), columns)
                    key_out[:, at] = ref[section, 0]
                    value_out[:, at] = ref[section, 1]

        memory_key_grad, memory_value_grad = call(
            assemble, lines, [(memory_key.shape, BF16), (memory_value.shape, BF16)]
        )

        def other_backward(*refs):
            received_ref, (stats, attended, lifted, weight, query) = refs[:1], refs[1:6]
            refs = refs[6:]
            values, stores = refs[:others], refs[others : 2 * others]
            pairs_out, slopes = refs[2 * others : 3 * others], refs[3 * others : 4 * others]
            grad_ref, scale_ref, delta_ref = refs[4 * others :]
            scale, delta, grad = norm_terms(received_ref, stats, attended, lifted, 0)
            scale_ref[...], delta_ref[...], grad_ref[...] = scale, delta, grad
            grad_tall = grad.astype(BF16)
            for by in range(others):
                line_weight = weight[by : by + 1, :]
                grad_folded = (grad * line_weight).astype(BF16)

                def key_grad(first, count, value, out=pairs_out[by]):
                    out[0, first : first + count, :] = value.astype(BF16)

                def value_grad(first, count, value, out=pairs_out[by]):
                    out[1, first : first + count, :] = value.astype(BF16)

                block_grads(
                    key_grad,
                    value_grad,
                    values[by],
                    stores[by],
                    line_weight,
                    delta,
                    grad_tall,
                    grad_folded,
                    query[...],
                    slopes[by],
                )

        results = call(
            other_backward,
            received
            + [self_stats, self_attended, self_lifted, other_weight, self_query]
            + other_values
            + list(other_stores),
            [((2,) + wide, BF16)] * others
            + [((frames, frames), BF16)] * others
            + [(tall, F32), (line, F32), (line, F32)],
            flops=3 * frames * unit * others,
            after=[cross_scale],
        )
        away, other_slopes = results[:others], results[others : 2 * others]
        self_attended_grad, self_scale, self_delta = results[2 * others :]
        home = [shifted(away[by], "ctx", contexts, -(by + 1)) for by in range(others)]

        def own_backward(grad, scale, delta, weight, gain, attended, query, key, value, store, *refs):
            keys, slopes = refs[:others], refs[others : 2 * others]
            key_out, value_out, query_out, out, own_slopes = refs[2 * others :]
            grad_tall = grad[...].astype(BF16)
            line_weight = weight[...]
            grad_folded = (grad[...] * line_weight).astype(BF16)

            def key_grad(first, count, result):
                key_out[first : first + count, :] = result

            def value_grad(first, count, result):
                value_out[first : first + count, :] = result

            block_grads(
                key_grad,
                value_grad,
                value,
                store,
                line_weight,
                delta[...],
                grad_tall,
                grad_folded,
                query[...],
                own_slopes,
            )
            total = dot_tn(key[...], own_slopes[...])
            for by in range(others):
                total = total + dot_tn(keys[by][...], slopes[by][...])
            query_out[...] = (total * scaling).T.astype(BF16)
            out[...] = (gain[...] * (attended[...] * scale[...]).T).astype(BF16)

        own_key, own_value, query_grad, self_out = call(
            own_backward,
            [
                self_attended_grad,
                self_scale,
                self_delta,
                first_weight,
                self_gain,
                self_attended,
                self_query,
                self_key,
                self_value,
                first_store,
            ]
            + other_keys
            + list(other_slopes),
            [(wide, F32), (wide, F32), (wide, BF16), (wide, BF16)],
            flops=(4 + others) * frames * unit,
            scratch=[pltpu.VMEM((frames, frames), BF16)],
        )

        def cross_rest(scale, gain, attended, *refs):
            blocks, slopes = refs[:contexts], refs[contexts : 2 * contexts]
            query_out, out = refs[2 * contexts :]
            total = dot_tn(blocks[0][0], slopes[0][...])
            for at in range(1, contexts):
                total = total + dot_tn(blocks[at][0], slopes[at][...])
            query_out[...] = (total * scaling).T.astype(BF16)
            out[...] = (gain[...] * (attended[...] * scale[...]).T).astype(BF16)

        cross_query_grad, cross_out = call(
            cross_rest,
            [cross_scale, cross_gain, cross_attended] + memories + list(cross_slopes),
            [(wide, BF16), (wide, BF16)],
            flops=group * contexts * unit,
        )

        def add_home(own_key_ref, own_value_ref, *refs):
            pairs, key_out, value_out = refs[:others], refs[others], refs[others + 1]
            for at, (own, out) in enumerate(((own_key_ref, key_out), (own_value_ref, value_out))):
                total = own[...]
                for pair in pairs:
                    total = total + pair[at].astype(F32)
                out[...] = total.astype(BF16)

        key_grad, value_grad = call(add_home, [own_key, own_value] + home, [(wide, BF16), (wide, BF16)])
        return (
            self_out,
            cross_out,
            query_grad,
            key_grad,
            value_grad,
            cross_query_grad,
            memory_key_grad,
            memory_value_grad,
        )

    rowed = P("ctx", ("sec", "tp"))
    stored = P(("sec", "ctx"), None)
    gains = P(("sec", "tp"))
    return jax.shard_map(
        per_device,
        mesh=mesh,
        in_specs=(rowed, rowed, rowed, gains, rowed, rowed, stored, stored, gains, rowed, P()),
        out_specs=(rowed, rowed, rowed, rowed, rowed, rowed, stored, stored),
        check_vma=False,
    )
```

```python
import math

import jax
import jax.numpy as jnp
from jax import lax
from jax.experimental import pallas as pl
from jax.experimental.pallas import tpu as pltpu
from jax.sharding import PartitionSpec as P


EPS = 1e-06
F32 = jnp.float32
BF16 = jnp.bfloat16
VMEM = pl.BlockSpec(memory_space=pltpu.VMEM)
ROOM = 4 << 20
LIMIT = 60 << 20
SMEM = pl.BlockSpec(memory_space=pltpu.SMEM)
HBM = pl.BlockSpec(memory_space=pltpu.HBM)


def call(body, inputs, outputs, flops=0, scratch=(), smem=0, after=(), loads=False):
    waits = len(after)
    if waits:
        inner, count = body, len(inputs)

        def body(*refs):
            inner(*refs[:count], *refs[count + waits :])

    moved = sum(math.prod(shape) * jnp.dtype(kind).itemsize for shape, kind in outputs)
    moved += sum(entry.size * entry.dtype.itemsize for entry in inputs)
    held = sum(
        math.prod(entry.shape) * jnp.dtype(entry.dtype).itemsize
        for entry in scratch
        if jnp.issubdtype(entry.dtype, jnp.number)
    )
    if loads:
        inputs = [pltpu.with_memory_space_constraint(entry, pltpu.HBM) for entry in inputs]
        shapes = [pltpu.VMEM(shape, kind) for shape, kind in outputs]
    else:
        shapes = [jax.ShapeDtypeStruct(shape, kind) for shape, kind in outputs]
    space = HBM if loads else VMEM
    return list(
        pl.pallas_call(
            body,
            out_shape=shapes,
            in_specs=[SMEM] * smem + [space] * (len(inputs) - smem) + [VMEM] * waits,
            out_specs=[VMEM] * len(outputs),
            scratch_shapes=list(scratch),
            cost_estimate=pl.CostEstimate(flops=flops, bytes_accessed=moved, transcendentals=0),
            compiler_params=pltpu.CompilerParams(
                vmem_limit_bytes=min(2 * (moved + held) + ROOM, LIMIT)
            ),
        )(*inputs, *after)
    )


def dot_nt(left, right):
    return lax.dot_general(left, right, (((1,), (1,)), ((), ())), preferred_element_type=F32)


def dot_nn(left, right):
    return lax.dot_general(left, right, (((1,), (0,)), ((), ())), preferred_element_type=F32)


def dot_tn(left, right):
    return lax.dot_general(left, right, (((0,), (0,)), ((), ())), preferred_element_type=F32)


def row_positions(bases, quarter):
    lanes = lax.broadcasted_iota(jnp.int32, (1, quarter), 1)
    parts = [bases[part : part + 1, part * quarter : (part + 1) * quarter] + lanes for part in range(4)]
    return jnp.concatenate(parts, axis=1)


def fold_scores(key, queries, running, store, masks, held, scaling):
    rows, step = key.shape[0], 128
    step = min(step, rows)
    top, total = running
    block_top = top
    for at in range(0, rows, step):
        scores = dot_nt(key[at : at + step, :], queries) * scaling
        if masks is not None:
            key_first, query_positions = masks
            down = lax.broadcasted_iota(jnp.int32, (step, 1), 0)
            scores = jnp.where(down > query_positions - key_first(at), -jnp.inf, scores)
        held[at : at + step, :] = scores
        block_max = jnp.max(scores, axis=0, keepdims=True)
        block_top = block_max if block_top is None else jnp.maximum(block_top, block_max)
    block_total = None
    for at in range(0, rows, step):
        raised = jnp.exp(held[at : at + step, :] - block_top)
        part = jnp.sum(raised, axis=0, keepdims=True)
        block_total = part if block_total is None else block_total + part
        store[at : at + step, :] = raised.astype(BF16)
    if top is not None:
        block_total = total * jnp.exp(top - block_top) + block_total
    return block_top, block_total


def solution(mesh):
    sections, contexts, tensors = mesh.shape["sec"], mesh.shape["ctx"], mesh.shape["tp"]
    peers = sections * tensors

    def shifted(value, axis, count, by):
        return lax.ppermute(value, axis, [(at, (at + by) % count) for at in range(count)])

    def paired(at, by, count):
        return jnp.bitwise_xor(at, by) if count & (count - 1) == 0 else lax.rem(at + by, count)

    def unpaired(at, by, count):
        return jnp.bitwise_xor(at, by) if count & (count - 1) == 0 else lax.rem(at - by + count, count)

    def swapped(value, axis, count, by, back=False):
        if count & (count - 1) == 0:
            return lax.ppermute(value, axis, [(at, at ^ by) for at in range(count)])
        return shifted(value, axis, count, -by if back else by)

    def over_sections(value, by, back=False):
        return swapped(value, "sec", sections, by, back)

    def over_tensors(value, by):
        return swapped(value, "tp", tensors, by)


    def per_device(
        self_query,
        self_key,
        self_value,
        self_gain,
        self_grad,
        cross_query,
        memory_key,
        memory_value,
        cross_gain,
        cross_grad,
        block_start,
    ):
        frames, columns = self_query.shape
        rows = memory_key.shape[0]
        quarter = frames // 4
        full_width = columns * peers
        group = sections * rows
        others = contexts - 1
        scaling = 1.0 / math.sqrt(columns)
        wide = (frames, columns)
        tall = (columns, frames)
        line = (1, frames)
        unit = 2 * frames * columns

        def copy_all(moves, semaphores, meanwhile=None):
            copies = [
                pltpu.make_async_copy(source, target, semaphores.at[at])
                for at, (source, target) in enumerate(moves)
            ]
            for copy in copies:
                copy.start()
            if meanwhile:
                meanwhile()
            for copy in copies:
                copy.wait()

        def load_memory(key_ref, value_ref, *refs):
            out, semaphores = refs
            section, tensor = lax.axis_index("sec"), lax.axis_index("tp")
            moves = []
            for by in range(sections):
                head = paired(section, by, sections) * tensors + tensor
                at = pl.ds(pl.multiple_of(head * columns, columns), columns)
                moves += [(key_ref.at[:, at], out.at[by, 0]), (value_ref.at[:, at], out.at[by, 1])]
            copy_all(moves, semaphores)

        (pieces,) = call(
            load_memory,
            [memory_key, memory_value],
            [((sections, 2, rows, columns), BF16)],
            scratch=[pltpu.SemaphoreType.DMA((2 * sections,))],
            loads=True,
        )

        plain = [
            self_query,
            self_key,
            self_value,
            self_grad,
            cross_query,
            cross_grad,
            self_gain.reshape(1, columns),
            cross_gain.reshape(1, columns),
        ]

        def load_rows(start_ref, *refs):
            count = len(plain)
            bases, starts, start_semaphore, semaphores = refs[-4:]
            first_copy = pltpu.make_async_copy(start_ref, starts, start_semaphore)
            first_copy.start()

            def positions():
                first_copy.wait()
                context = lax.axis_index("ctx")
                for by in range(contexts):
                    source = lax.rem(context - by + contexts, contexts)
                    for part in range(4):
                        at = by * 4 + part
                        first = starts[source * 4 + part] * quarter
                        bases[at : at + 1, :] = jnp.full((1, frames), first, jnp.int32)

            copy_all(list(zip(refs[:count], refs[count : 2 * count])), semaphores, positions)

        other_keys = [shifted(self_key, "ctx", contexts, by) for by in range(1, contexts)]
        other_values = [shifted(self_value, "ctx", contexts, by) for by in range(1, contexts)]

        results = call(
            load_rows,
            [block_start] + plain,
            [(entry.shape, entry.dtype) for entry in plain] + [((4 * contexts, frames), jnp.int32)],
            scratch=[
                pltpu.SMEM(block_start.shape, jnp.int32),
                pltpu.SemaphoreType.DMA,
                pltpu.SemaphoreType.DMA((len(plain),)),
            ],
            loads=True,
        )
        self_query, self_key, self_value, self_grad, cross_query, cross_grad, self_gain, cross_gain, bases = results

        blocks_in = [pieces] + [shifted(pieces, "ctx", contexts, by) for by in range(1, contexts)]

        def regroup(*refs):
            ins, outs = refs[:contexts], refs[contexts:]
            for by, out in enumerate(outs):
                for at, ref in enumerate(ins):
                    out[at] = ref[by]

        packs = call(regroup, blocks_in, [((contexts, 2, rows, columns), BF16)] * sections)
        arrived = [packs[0]] + [over_sections(packs[by], by) for by in range(1, sections)]

        def gather(*refs):
            ins, outs = refs[:sections], refs[sections:]
            for at, out in enumerate(outs):
                for by, ref in enumerate(ins):
                    out[:, by * rows : (by + 1) * rows, :] = ref[at]

        memories = call(gather, arrived, [((2, group, columns), BF16)] * contexts)

        def first_block(
            base,
            query,
            key,
            value,
            gain,
            grad,
            cross_gain_ref,
            cross_grad_ref,
            store,
            top,
            total,
            weighted,
            lifted,
            cross_lifted_ref,
            held,
        ):
            masks = (
                lambda at: base[at // quarter : at // quarter + 1, :] + at % quarter,
                row_positions(base, quarter),
            )
            top[...], total[...] = fold_scores(
                key, query[...], (None, None), store, masks, held, scaling
            )
            weighted[...] = dot_tn(value[...], store[...])
            lifted[...] = (gain[...] * grad[...].astype(F32)).T
            cross_lifted_ref[...] = (cross_gain_ref[...] * cross_grad_ref[...].astype(F32)).T

        first_store, first_top, first_total, first_weighted, self_lifted, cross_lifted = call(
            first_block,
            [
                bases,
                self_query,
                self_key,
                self_value,
                self_gain,
                self_grad,
                cross_gain,
                cross_grad,
            ],
            [((frames, frames), BF16), (line, F32), (line, F32), (tall, F32), (tall, F32), (tall, F32)],
            flops=2 * frames * unit,
            scratch=[pltpu.VMEM((frames, frames), F32)],
        )

        def statistics(attended, lifted):
            return (
                jnp.sum(attended * attended, axis=0, keepdims=True),
                jnp.sum(lifted * attended, axis=0, keepdims=True),
            )

        def other_scores(base, query, top, total, *refs):
            keys, stores = refs[:others], refs[others : 2 * others]
            first_weight, weight, held = refs[2 * others :]
            positions = row_positions(base, quarter)
            running = (top[...], total[...])
            tops = [top[...]]
            for by in range(others):
                first = 4 * (by + 1)
                masks = (
                    lambda at, first=first: base[first + at // quarter : first + at // quarter + 1, :]
                    + at % quarter,
                    positions,
                )
                running = fold_scores(keys[by], query[...], running, stores[by], masks, held, scaling)
                tops.append(running[0])
            last = 1.0 / running[1]
            first_weight[...] = jnp.exp(tops[0] - running[0]) * last
            for by in range(others):
                weight[by : by + 1, :] = jnp.exp(tops[by + 1] - running[0]) * last

        results = call(
            other_scores,
            [bases, self_query, first_top, first_total] + other_keys,
            [((frames, frames), BF16)] * others + [(line, F32), ((others, frames), F32)],
            flops=frames * unit * others,
            scratch=[pltpu.VMEM((frames, frames), F32)],
        )
        other_stores, (first_weight, other_weight) = results[:others], results[others:]

        def cross_forward(query, lifted, *refs):
            blocks, stores = refs[:contexts], refs[contexts : 2 * contexts]
            weight, attended_ref, stats, held = refs[2 * contexts :]
            running = (None, None)
            tops = []
            for at in range(contexts):
                running = fold_scores(blocks[at].at[0], query[...], running, stores[at], None, held, scaling)
                tops.append(running[0])
            last = 1.0 / running[1]
            attended = None
            for at in range(contexts):
                factor = jnp.exp(tops[at] - running[0]) * last
                weight[at : at + 1, :] = factor
                part = dot_tn(blocks[at][1], stores[at][...]) * factor
                attended = part if attended is None else attended + part
            attended_ref[...] = attended
            stats[0:1, :], stats[1:2, :] = statistics(attended, lifted[...])

        results = call(
            cross_forward,
            [cross_query, cross_lifted] + memories,
            [((group, frames), BF16)] * contexts
            + [
                ((contexts, frames), F32),
                (tall, F32),
                ((2, frames), F32),
            ],
            flops=2 * group * contexts * unit,
            scratch=[pltpu.VMEM((group, frames), F32)],
        )
        cross_stores = results[:contexts]
        cross_weight, cross_attended, cross_stats = results[contexts:]

        half = frames // 2

        def other_values_seen(weighted, first_weight_ref, weight, lifted, cross_stats_ref, *refs):
            values, stores = refs[:others], refs[others : 2 * others]
            attended_ref, packed = refs[2 * others :]
            attended = weighted[...] * first_weight_ref[...]
            for by in range(others):
                attended = attended + dot_tn(values[by][...], stores[by][...]) * weight[by : by + 1, :]
            attended_ref[...] = attended
            squares, slopes = statistics(attended, lifted[...])
            lines = [squares, slopes, cross_stats_ref[0:1, :], cross_stats_ref[1:2, :]]
            halves = [entry[:, at : at + half] for entry in lines for at in (0, half)]
            tile = jnp.concatenate(halves, axis=0)
            for at in range(peers):
                packed[at] = tile.astype(BF16)

        self_attended, packed = call(
            other_values_seen,
            [first_weighted, first_weight, other_weight, self_lifted, cross_stats] + other_values + other_stores,
            [(tall, F32), ((peers, 8, half), BF16)],
            flops=frames * unit * others,
        )


        received = [lax.all_to_all(packed, ("sec", "tp"), split_axis=0, concat_axis=0, tiled=True)]

        def norm_terms(received_ref, attended, lifted, at):
            sums = received_ref[0][0].astype(F32)
            for source in range(1, peers):
                sums = sums + received_ref[0][source].astype(F32)
            joined = [
                jnp.concatenate([sums[2 * pick : 2 * pick + 1], sums[2 * pick + 1 : 2 * pick + 2]], axis=1)
                for pick in (2 * at, 2 * at + 1)
            ]
            scale = lax.rsqrt(joined[0] / full_width + EPS)
            slope = joined[1] / full_width
            curve = scale * scale * slope
            grad = scale * (lifted[...] - attended[...] * curve)
            rounded = grad.astype(BF16).astype(F32)
            delta = jnp.sum(rounded * attended[...], axis=0, keepdims=True)
            return scale, delta, grad

        def block_grads(key_grad, value_grad, value, store, weight, delta, grad_tall, grad_folded, query, slopes):
            count, step = value.shape[0], 128
            step = min(step, count)
            for at in range(0, count, step):
                products = dot_nn(value[at : at + step, :], grad_tall)
                probs = store[at : at + step, :]
                slope = (probs.astype(F32) * ((products - delta) * weight)).astype(BF16)
                slopes[at : at + step, :] = slope
                key_grad(at, step, dot_nn(slope, query) * scaling)
                value_grad(at, step, dot_nt(probs, grad_folded))

        def memory_grads(block, store, factor, delta, grad, query, out, slopes):
            grad_folded = (grad * factor).astype(BF16)

            def key_grad(first, count, value):
                out[0, first : first + count, :] = value.astype(out.dtype)

            def value_grad(first, count, value):
                out[1, first : first + count, :] = value.astype(out.dtype)

            block_grads(
                key_grad,
                value_grad,
                block.at[1],
                store,
                factor,
                delta,
                grad.astype(BF16),
                grad_folded,
                query[...],
                slopes,
            )

        def cross_backward(*refs):
            received_ref, (attended, lifted, weight, query) = refs[:1], refs[1:5]
            refs = refs[5:]
            blocks, stores = refs[:others], refs[others : 2 * others]
            sums, slopes = refs[2 * others : 3 * others], refs[3 * others : 4 * others]
            scale_ref, delta_ref, grad_ref = refs[4 * others :]
            scale, delta, grad = norm_terms(received_ref, attended, lifted, 1)
            scale_ref[...], delta_ref[...], grad_ref[...] = scale, delta, grad
            for by in range(others):
                factor = weight[by + 1 : by + 2, :]
                memory_grads(blocks[by], stores[by], factor, delta, grad, query, sums[by], slopes[by])

        results = call(
            cross_backward,
            received
            + [cross_attended, cross_lifted, cross_weight, cross_query]
            + memories[1:]
            + cross_stores[1:],
            [((2, group, columns), BF16)] * others
            + [((group, frames), BF16)] * others
            + [(line, F32), (line, F32), (tall, F32)],
            flops=3 * group * others * unit,
        )
        away_sums, away_slopes = results[:others], results[others : 2 * others]
        cross_scale, cross_delta, cross_attended_grad = results[2 * others :]

        def cross_own(delta, grad, weight, query, block, store, out, slopes):
            memory_grads(block, store, weight[0:1, :], delta[...], grad[...], query, out, slopes)

        own_sums, own_slopes_cross = call(
            cross_own,
            [cross_delta, cross_attended_grad, cross_weight, cross_query, memories[0], cross_stores[0]],
            [((2, group, columns), F32), ((group, frames), BF16)],
            flops=3 * group * unit,
        )
        cross_slopes = [own_slopes_cross] + away_slopes

        returned = [shifted(away_sums[by], "ctx", contexts, -(by + 1)) for by in range(others)]

        def add_up(*refs):
            own, extra, outs = refs[0], refs[1 : 1 + others], refs[1 + others :]
            for at, out in enumerate(outs):
                part = slice(at * rows, (at + 1) * rows)
                total = own[:, part, :]
                for entry in extra:
                    total = total + entry[:, part, :].astype(F32)
                out[...] = total.astype(BF16)

        parts = call(add_up, [own_sums] + returned, [((2, rows, columns), BF16)] * sections)
        back = [parts[0]] + [over_sections(parts[by], by, back=True) for by in range(1, sections)]

        def by_section(*refs):
            out = refs[-1]
            section = lax.axis_index("sec")
            for by, ref in enumerate(refs[:-1]):
                out[paired(section, by, sections)] = ref[...]

        (mine,) = call(by_section, back, [((sections, 2, rows, columns), BF16)])
        lines = [mine] + [over_tensors(mine, by) for by in range(1, tensors)]

        def assemble(*refs):
            sources, key_out, value_out = refs[:tensors], refs[tensors], refs[tensors + 1]
            tensor = lax.axis_index("tp")
            for by, ref in enumerate(sources):
                source = unpaired(tensor, by, tensors)
                for section in range(sections):
                    head = section * tensors + source
                    at = pl.ds(pl.multiple_of(head * columns, columns), columns)
                    key_out[:, at] = ref[section, 0]
                    value_out[:, at] = ref[section, 1]

        memory_key_grad, memory_value_grad = call(
            assemble, lines, [(memory_key.shape, BF16), (memory_value.shape, BF16)]
        )

        def other_backward(*refs):
            received_ref, (attended, lifted, weight, query) = refs[:1], refs[1:5]
            refs = refs[5:]
            values, stores = refs[:others], refs[others : 2 * others]
            pairs_out, slopes = refs[2 * others : 3 * others], refs[3 * others : 4 * others]
            grad_ref, scale_ref, delta_ref = refs[4 * others :]
            scale, delta, grad = norm_terms(received_ref, attended, lifted, 0)
            scale_ref[...], delta_ref[...], grad_ref[...] = scale, delta, grad
            grad_tall = grad.astype(BF16)
            for by in range(others):
                line_weight = weight[by : by + 1, :]
                grad_folded = (grad * line_weight).astype(BF16)

                def key_grad(first, count, value, out=pairs_out[by]):
                    out[0, first : first + count, :] = value.astype(BF16)

                def value_grad(first, count, value, out=pairs_out[by]):
                    out[1, first : first + count, :] = value.astype(BF16)

                block_grads(
                    key_grad,
                    value_grad,
                    values[by],
                    stores[by],
                    line_weight,
                    delta,
                    grad_tall,
                    grad_folded,
                    query[...],
                    slopes[by],
                )

        results = call(
            other_backward,
            received
            + [self_attended, self_lifted, other_weight, self_query]
            + other_values
            + list(other_stores),
            [((2,) + wide, BF16)] * others
            + [((frames, frames), BF16)] * others
            + [(tall, F32), (line, F32), (line, F32)],
            flops=3 * frames * unit * others,
            after=[cross_scale],
        )
        away, other_slopes = results[:others], results[others : 2 * others]
        self_attended_grad, self_scale, self_delta = results[2 * others :]
        home = [shifted(away[by], "ctx", contexts, -(by + 1)) for by in range(others)]

        def own_backward(grad, scale, delta, weight, gain, attended, query, key, value, store, *refs):
            keys, slopes = refs[:others], refs[others : 2 * others]
            key_out, value_out, query_out, out, own_slopes = refs[2 * others :]
            grad_tall = grad[...].astype(BF16)
            line_weight = weight[...]
            grad_folded = (grad[...] * line_weight).astype(BF16)

            def key_grad(first, count, result):
                key_out[first : first + count, :] = result

            def value_grad(first, count, result):
                value_out[first : first + count, :] = result

            block_grads(
                key_grad,
                value_grad,
                value,
                store,
                line_weight,
                delta[...],
                grad_tall,
                grad_folded,
                query[...],
                own_slopes,
            )
            total = dot_tn(key[...], own_slopes[...])
            for by in range(others):
                total = total + dot_tn(keys[by][...], slopes[by][...])
            query_out[...] = (total * scaling).T.astype(BF16)
            out[...] = (gain[...] * (attended[...] * scale[...]).T).astype(BF16)

        own_key, own_value, query_grad, self_out = call(
            own_backward,
            [
                self_attended_grad,
                self_scale,
                self_delta,
                first_weight,
                self_gain,
                self_attended,
                self_query,
                self_key,
                self_value,
                first_store,
            ]
            + other_keys
            + list(other_slopes),
            [(wide, F32), (wide, F32), (wide, BF16), (wide, BF16)],
            flops=(4 + others) * frames * unit,
            scratch=[pltpu.VMEM((frames, frames), BF16)],
        )

        def cross_rest(scale, gain, attended, *refs):
            blocks, slopes = refs[:contexts], refs[contexts : 2 * contexts]
            query_out, out = refs[2 * contexts :]
            total = dot_tn(blocks[0][0], slopes[0][...])
            for at in range(1, contexts):
                total = total + dot_tn(blocks[at][0], slopes[at][...])
            query_out[...] = (total * scaling).T.astype(BF16)
            out[...] = (gain[...] * (attended[...] * scale[...]).T).astype(BF16)

        cross_query_grad, cross_out = call(
            cross_rest,
            [cross_scale, cross_gain, cross_attended] + memories + list(cross_slopes),
            [(wide, BF16), (wide, BF16)],
            flops=group * contexts * unit,
        )

        def add_home(own_key_ref, own_value_ref, *refs):
            pairs, key_out, value_out = refs[:others], refs[others], refs[others + 1]
            for at, (own, out) in enumerate(((own_key_ref, key_out), (own_value_ref, value_out))):
                total = own[...]
                for pair in pairs:
                    total = total + pair[at].astype(F32)
                out[...] = total.astype(BF16)

        key_grad, value_grad = call(add_home, [own_key, own_value] + home, [(wide, BF16), (wide, BF16)])
        return (
            self_out,
            cross_out,
            query_grad,
            key_grad,
            value_grad,
            cross_query_grad,
            memory_key_grad,
            memory_value_grad,
        )

    rowed = P("ctx", ("sec", "tp"))
    stored = P(("sec", "ctx"), None)
    gains = P(("sec", "tp"))
    return jax.shard_map(
        per_device,
        mesh=mesh,
        in_specs=(rowed, rowed, rowed, gains, rowed, rowed, stored, stored, gains, rowed, P()),
        out_specs=(rowed, rowed, rowed, rowed, rowed, rowed, stored, stored),
        check_vma=False,
    )
```
